128 devices in a mesh: colour: 2 (over core), sub: 64 (over z, y, x).
Axes of the slice: x: 4, y: 4, z: 4, core: 2. Of those that a mesh axis runs over, the one named last changes fastest.
Arguments:
- rhs: float32 [3, 256, 256, 512], P(None, 'sub'), may hold values from -60 to 60
- diagonal: float32 [256, 256, 512], P('sub'), may hold values from 0.2 to 6
Outputs:
- solution: float32 [3, 256, 256, 512], P(None, 'sub', None, 'colour')
- residual: float32 [3, 256, 256, 512], P(None, 'sub', None, 'colour')
- norms: float32 [3], replicated
The draws below stay inside these ranges and needn't reach their ends.
All inputs are finite; a program needn't handle non-finite values.
Results may differ from the reference program's by a relative error of at most 0.0003.
Values sent between devices are 32-bit elements; how exact they have to be, the bound alone decides.
No kernel may reach another device: no remote copies, remote signals or barrier semaphores. Data moves between devices by JAX's collectives and lax.ppermute only.
A program may use at most 128 MiB of HBM per device.

```python
import math
import jax
import jax.numpy as jnp
from jax import lax

CX = 4
NY = 256
NZ = 512
RIM = 1
SWEEPS = 8
NRHS = 3
NX = 256
N_SUB = 64


def draw_rhs(key, part):
    first = jax.random.fold_in(jax.random.fold_in(key, 17), 0)
    base = jax.random.normal(first, (NRHS, NX, NY, NZ), jnp.float32)
    ramp = 1.0 + 2.0 * jnp.arange(NX, dtype=jnp.float32) / (NX - 1)
    ramp = ramp[None, :, None, None]
    field = base * ramp
    return jnp.clip(field, -60.0, 60.0)


def level_of(rng, extent, shards, low, largest):
    gain = 1.0
    for axis_at, parts in shards:
        steps = jax.random.uniform(jax.random.fold_in(jax.random.fold_in(rng, 6), axis_at), (parts,), jnp.float32, low / len(shards), largest / len(shards))
        gain = gain * jnp.repeat(jnp.exp(steps), extent[axis_at] // parts).reshape((-1,) + (1,) * (len(extent) - 1 - axis_at))
    return gain


def setup_inputs(seed: int = 0) -> dict:
    seeds = jax.random.split(jax.random.key(seed), 3)
    return {
        "rhs": draw_rhs(jax.random.fold_in(seeds[2], 71), 0),
        "diagonal": jnp.clip(jnp.exp(math.log(6.0) - 3.4011974 * jax.random.uniform(seeds[1], (NX, NY, NZ), jnp.float32) ** level_of(seeds[1], (NX, NY, NZ), ((0, 64),), -0.2, 0.2)), 0.2, 6.0),
    }


OMEGA = 0.8

def neighbours(field):
    pads = ((0, 0),) * (field.ndim - 3) + ((1, 1), (1, 1), (1, 1))
    padded = jnp.pad(field, pads)
    beside = padded[..., 2:, 1:-1, 1:-1] + padded[..., :-2, 1:-1, 1:-1]
    beside = beside + padded[..., 1:-1, 2:, 1:-1] + padded[..., 1:-1, :-2, 1:-1]
    beside = beside + padded[..., 1:-1, 1:-1, 2:] + padded[..., 1:-1, 1:-1, :-2]
    return beside

def jacobi(resid, diag, mask):
    scale = OMEGA / (6.0 + diag)
    found = jnp.zeros_like(resid)
    for sweep in range(SWEEPS):
        found = (found + scale * (resid - (6.0 + diag) * found + neighbours(found))) * mask
    return found

def operate(field, diagonal):
    return (6.0 + diagonal) * field - neighbours(field)

def reference(rhs, diagonal):
    half = CX // 2
    span = half + 2 * RIM
    padded_diag = jnp.pad(diagonal, ((RIM, RIM), (0, 0), (0, 0)))
    layouts = []
    for colour in range(2):
        starts = jnp.arange(N_SUB, dtype=jnp.int32) * CX + colour * half
        index = (starts[:, None] + jnp.arange(span, dtype=jnp.int32)[None, :]).astype(jnp.int32)
        place = index - RIM
        mask = ((place >= 0) & (place < NX)).astype(jnp.float32)[:, :, None, None]
        layouts.append((index, mask, padded_diag[index]))

    def correction(resid, layout):
        index, mask, diag_regions = layout
        padded = jnp.pad(resid, ((RIM, RIM), (0, 0), (0, 0)))
        regions = padded[index] * mask
        found = jacobi(regions, diag_regions, mask)
        total = jnp.zeros_like(padded).at[index.reshape(-1)].add(found.reshape(-1, NY, NZ))
        return total[RIM:RIM + NX]

    def one_rhs(source):
        current = jnp.zeros_like(source)
        resid = source
        for colour in range(2):
            corr = correction(resid, layouts[colour])
            image = operate(corr, diagonal)
            alpha = jnp.sum(resid * corr) / jnp.sum(corr * image)
            current = current + alpha * corr
            resid = resid - alpha * image
        return (current, resid, jnp.sqrt(jnp.sum(resid * resid)))
    solution, residual, norms = lax.map(one_rhs, rhs)
    return (solution, residual, norms)
```

```python
import functools

import jax
import jax.numpy as jnp
from jax import lax
from jax.experimental import pallas as pl
from jax.experimental.pallas import tpu as pltpu
from jax.sharding import Mesh
from jax.sharding import PartitionSpec as P

OMEGA = 0.8
SWEEPS = 8
NY = 256
NZ = 512
NRHS = 3
OWN = 128
WIN = 144
K = WIN // 8
LANES = 128
TILES = NZ // LANES
SUB = ("sub_0", "sub_1", "sub_2")
VMEM_LIMIT = 32 * 1024 * 1024


def powers():
    total = [0.0] * SWEEPS
    power = [1.0]
    for _ in range(SWEEPS):
        for i, value in enumerate(power):
            total[i] += value
        longer = [0.0] * (len(power) + 1)
        for i, value in enumerate(power):
            longer[i] += (1.0 - OMEGA) * value
            longer[i + 1] += value
        power = longer
    return total


COEFFICIENTS = powers()
PLANE = (K, 8, NZ)


def shape_of(*lead):
    return jax.ShapeDtypeStruct((*lead, *PLANE), jnp.float32)


def tile(t):
    return slice(t * LANES, (t + 1) * LANES)


def lanes():
    return lax.broadcasted_iota(jnp.int32, (8, LANES), 1)


def sublanes():
    return lax.broadcasted_iota(jnp.int32, (8, LANES), 0)


def owned(k, colour):
    row = sublanes() * K + k - colour * (WIN - OWN)
    return (row >= 0) & (row < OWN)


def close_edges(buf):
    sub = sublanes()
    for p in range(4):
        for t in range(TILES):
            last = pltpu.roll(buf[p, K, :, tile(t)], 1, 0)
            buf[p, 0, :, tile(t)] = jnp.where(sub == 0, 0.0, last)
            first = pltpu.roll(buf[p, 1, :, tile(t)], 7, 0)
            buf[p, K + 1, :, tile(t)] = jnp.where(sub == 7, 0.0, first)


def beside(buf, k):
    lane = lanes()
    first, last = lane == 0, lane == LANES - 1
    here = [[buf[p, k + 1, :, tile(t)] for t in range(TILES)] for p in range(4)]
    sums = []
    for p in range(4):
        up = [pltpu.roll(v, 1, 1) for v in here[p]]
        down = [pltpu.roll(v, LANES - 1, 1) for v in here[p]]
        row = []
        for t in range(TILES):
            total = jnp.where(first, up[t - 1] if t else 0.0, up[t])
            total = total + jnp.where(last, down[t + 1] if t + 1 < TILES else 0.0, down[t])
            total = total + (buf[p, k, :, tile(t)] + buf[p, k + 2, :, tile(t)])
            if p == 0:
                total = total + here[1][t]
            elif p == 3:
                total = total + here[2][t]
            else:
                total = total + (here[p - 1][t] + here[p + 1][t])
            row.append(total)
        sums.append(row)
    return sums, here


def solve(source, scale, one, two):
    close_edges(one)
    bufs = (one, two)
    for step, power in enumerate(range(SWEEPS - 2, -1, -1)):
        src, dst = bufs[step % 2], bufs[1 - step % 2]
        factor = COEFFICIENTS[power]

        def body(k, _, src=src, dst=dst, factor=factor):
            sums, _ = beside(src, k)
            for p in range(4):
                for t in range(TILES):
                    dst[p, k + 1, :, tile(t)] = (
                        scale[p, k, :, tile(t)] * sums[p][t]
                        + factor * source[p, k, :, tile(t)]
                    )
            return 0

        lax.fori_loop(0, K, body, 0)
        close_edges(dst)
    return bufs[(SWEEPS - 1) % 2]


def prepare_kernel(planes, at, *refs):
    where, rhs, diag = at, refs[0], refs[1]
    count = NRHS + 1
    outs = refs[2 : 2 + len(planes) * count]
    held, sem = refs[2 + len(planes) * count :]
    low = pl.multiple_of(where[0] * (NY - WIN), 8)
    copies = []
    for i, plane in enumerate(planes):
        for r in range(count):
            for t in range(TILES):
                if r < NRHS:
                    src = rhs.at[r, plane, pl.ds(low, WIN), tile(t)]
                else:
                    src = diag.at[plane, pl.ds(low, WIN), tile(t)]
                copies.append(
                    pltpu.make_async_copy(src, held.at[i * count + r, t], sem.at[i * count + r, t])
                )
    for copy in copies:
        copy.start()
    for n, out in enumerate(outs):
        for t in range(TILES):
            copies[n * TILES + t].wait()
            for k in range(K):
                out[k, :, tile(t)] = held[n, t, pl.ds(k, 8, stride=K), :]


def prepare(planes, where, rhs, diag):
    count = len(planes) * (NRHS + 1)
    return pl.pallas_call(
        functools.partial(prepare_kernel, planes),
        out_shape=[shape_of()] * count,
        in_specs=[
            pl.BlockSpec(memory_space=pltpu.SMEM),
            pl.BlockSpec(memory_space=pl.ANY),
            pl.BlockSpec(memory_space=pl.ANY),
        ],
        out_specs=[pl.BlockSpec(memory_space=pltpu.VMEM)] * count,
        scratch_shapes=[
            pltpu.VMEM((count, TILES, WIN, LANES), jnp.float32),
            pltpu.SemaphoreType.DMA((count, TILES)),
        ],
        compiler_params=pltpu.CompilerParams(vmem_limit_bytes=VMEM_LIMIT),
        cost_estimate=pl.CostEstimate(flops=0, bytes_accessed=count * 600000, transcendentals=0),
    )(where, rhs, diag)


def local(buf, diags, k):
    sums, here = beside(buf, k)
    images = [
        [(6.0 + diags[p][k, :, tile(t)]) * here[p][t] - sums[p][t] for t in range(TILES)]
        for p in range(4)
    ]
    return images, here


def fill(k, p, q, d, keep, scale, source, one):
    for t in range(TILES):
        s = OMEGA / (6.0 + d[k, :, tile(t)])
        if keep is not None:
            s = s * keep
        g = s * q[t]
        scale[p, k, :, tile(t)] = s
        source[p, k, :, tile(t)] = g
        one[p, k + 1, :, tile(t)] = g


SCRATCH = [
    pltpu.VMEM((4, K, 8, NZ), jnp.float32),
    pltpu.VMEM((4, K, 8, NZ), jnp.float32),
    pltpu.VMEM((4, K + 2, 8, NZ), jnp.float32),
    pltpu.VMEM((4, K + 2, 8, NZ), jnp.float32),
]


def first_kernel(where, qh, q0, q1, q2, dh, d0, d1, d2, ch, c, t2, t12, sums, scale, source, one, two):
    colour, device = where[0], where[1]
    keep = (device > 0).astype(jnp.float32)
    qs, ds = (qh, q0, q1, q2), (dh, d0, d1, d2)

    def start(k, _):
        for p in range(4):
            q = [qs[p][k, :, tile(t)] for t in range(TILES)]
            fill(k, p, q, ds[p], keep if p == 0 else None, scale, source, one)
        return 0

    lax.fori_loop(0, K, start, 0)
    found = solve(source, scale, one, two)

    def finish(k, carry):
        upper, lower = carry
        images, here = local(found, ds, k)
        mask = owned(k, colour)
        up, low = 0.0, 0.0
        for p in range(4):
            for t in range(TILES):
                value = here[p][t]
                up = up + qs[p][k, :, tile(t)] * value
                low = low + images[p][t] * value
                if p == 0:
                    ch[k, :, tile(t)] = value
                else:
                    c[p - 1, k, :, tile(t)] = value
                if p < 2:
                    t2[p, k, :, tile(t)] = images[p][t]
                else:
                    t12[p - 2, k, :, tile(t)] = images[p][t]
        return upper + jnp.where(mask, up, 0.0), lower + jnp.where(mask, low, 0.0)

    zero = jnp.zeros((8, LANES), jnp.float32)
    upper, lower = lax.fori_loop(0, K, finish, (zero, zero))
    sums[0] = upper
    sums[1] = lower


VM = pl.BlockSpec(memory_space=pltpu.VMEM)
SM = pl.BlockSpec(memory_space=pltpu.SMEM)


def estimate(planes, passes):
    return pl.CostEstimate(
        flops=passes * 4 * K * 8 * NZ * 10, bytes_accessed=planes * K * 8 * NZ * 4, transcendentals=0
    )


def first_solve(where, *arrays):
    return pl.pallas_call(
        first_kernel,
        out_shape=[
            shape_of(),
            shape_of(3),
            shape_of(2),
            shape_of(2),
            jax.ShapeDtypeStruct((2, 8, LANES), jnp.float32),
        ],
        in_specs=[SM] + [VM] * 8,
        out_specs=[VM] * 5,
        scratch_shapes=SCRATCH,
        compiler_params=pltpu.CompilerParams(vmem_limit_bytes=VMEM_LIMIT),
        cost_estimate=estimate(16, SWEEPS + 1),
    )(where, *arrays)


def rows_of(values, count):
    rows = [jnp.sum(v, axis=0, keepdims=True) for v in values]
    rows += [jnp.zeros((1, LANES), jnp.float32)] * (count - len(rows))
    return jnp.concatenate(rows, axis=0)


def join_kernel(where, *refs):
    cs, rights, sums, out = refs[:NRHS], refs[NRHS : 2 * NRHS], refs[2 * NRHS : 3 * NRHS], refs[-1]
    colour = where[0]
    zero = jnp.zeros((8, LANES), jnp.float32)
    uppers, lowers = [], []
    for r in range(NRHS):

        def body(k, total, r=r):
            add = 0.0
            for t in range(TILES):
                add = add + cs[r][2, k, :, tile(t)] * rights[r][k, :, tile(t)]
            return total + jnp.where(owned(k, colour), add, 0.0)

        between = lax.fori_loop(0, K, body, zero)
        uppers.append(sums[r][0])
        lowers.append(sums[r][1] - 2.0 * between)
    out[...] = rows_of(uppers + lowers, 8)


def join(where, cs, rights, sums):
    return pl.pallas_call(
        join_kernel,
        out_shape=jax.ShapeDtypeStruct((8, LANES), jnp.float32),
        in_specs=[SM] + [VM] * (3 * NRHS),
        out_specs=VM,
        compiler_params=pltpu.CompilerParams(vmem_limit_bytes=VMEM_LIMIT),
        cost_estimate=estimate(12, 1),
    )(where, *cs, *rights, *sums)


def ratio(table, upper, lower):
    top = jnp.sum(table[upper : upper + 1, :], axis=1, keepdims=True)
    bottom = jnp.sum(table[lower : lower + 1, :], axis=1, keepdims=True)
    return top / bottom


def second_kernel(
    r, where, table, q1, q2, q3, q4, d1, d2, d3, d4, c, cr, tr, t12,
    ca, cm, cd, ta, tm, td, res, sums, scale, source, one, two,
):
    colour, device, count = where[0], where[1], where[2]
    keep = (device < count - 1).astype(jnp.float32)
    alpha = jnp.broadcast_to(ratio(table, r, NRHS + r), (8, LANES))
    ds = (d1, d2, d3, d4)

    def start(k, _):
        for p in range(4):
            values = []
            for t in range(TILES):
                if p == 0:
                    image = t12[0, k, :, tile(t)]
                    q = q1[k, :, tile(t)]
                elif p == 1:
                    image = t12[1, k, :, tile(t)] - cr[k, :, tile(t)]
                    q = q2[k, :, tile(t)]
                elif p == 2:
                    image = tr[0, k, :, tile(t)] - c[2, k, :, tile(t)]
                    q = q3[k, :, tile(t)]
                else:
                    image = tr[1, k, :, tile(t)]
                    q = q4[k, :, tile(t)]
                value = q - alpha * image
                res[p, k, :, tile(t)] = value
                values.append(value)
            fill(k, p, values, ds[p], keep if p == 3 else None, scale, source, one)
        return 0

    lax.fori_loop(0, K, start, 0)
    found = solve(source, scale, one, two)

    def finish(k, carry):
        images, here = local(found, ds, k)
        mask = owned(k, colour)
        adds = [0.0] * 5
        for p in range(4):
            for t in range(TILES):
                value, image, q = here[p][t], images[p][t], res[p, k, :, tile(t)]
                adds[0] = adds[0] + q * value
                adds[1] = adds[1] + image * value
                if p in (1, 2):
                    rest = q - image
                    adds[2] = adds[2] + rest * rest
                    adds[3] = adds[3] + rest * image
                    adds[4] = adds[4] + image * image
                    cm[p - 1, k, :, tile(t)] = value
                    tm[p - 1, k, :, tile(t)] = image
                else:
                    (ca if p == 0 else cd)[k, :, tile(t)] = value
                    (ta if p == 0 else td)[k, :, tile(t)] = image
        return tuple(a + jnp.where(mask, b, 0.0) for a, b in zip(carry, adds))

    zero = jnp.zeros((8, LANES), jnp.float32)
    found_sums = lax.fori_loop(0, K, finish, (zero,) * 5)
    for i in range(5):
        sums[i] = found_sums[i]


def second_solve(r, where, table, *arrays):
    return pl.pallas_call(
        functools.partial(second_kernel, r),
        out_shape=[
            shape_of(),
            shape_of(2),
            shape_of(),
            shape_of(),
            shape_of(2),
            shape_of(),
            shape_of(4),
            jax.ShapeDtypeStruct((5, 8, LANES), jnp.float32),
        ],
        in_specs=[SM] + [VM] * 13,
        out_specs=[VM] * 8,
        scratch_shapes=SCRATCH,
        compiler_params=pltpu.CompilerParams(vmem_limit_bytes=VMEM_LIMIT),
        cost_estimate=estimate(28, SWEEPS + 1),
    )(where, table, *arrays)


def join_second_kernel(where, table, *refs):
    out = refs[-1]
    colour, device, count = where[0], where[1], where[2]
    begin = (device == 0).astype(jnp.float32)
    inside = (device < count - 1).astype(jnp.float32)
    zero = jnp.zeros((8, LANES), jnp.float32)
    rows = [[] for _ in range(5)]
    for r in range(NRHS):
        res, ca, cd, ta, td, cl, cr, q0, t2, sums = refs[10 * r : 10 * r + 10]
        alpha = jnp.broadcast_to(ratio(table, r, NRHS + r), (8, LANES))

        def body(k, carry, res=res, ca=ca, cd=cd, ta=ta, td=td, cl=cl, cr=cr, q0=q0, t2=t2, alpha=alpha):
            between = 0.0
            parts = [[0.0] * 3 for _ in range(3)]
            for t in range(TILES):
                at = (k, slice(None), tile(t))
                between = between + ca[at] * cl[at] + cd[at] * cr[at]
                for n, (q, image) in enumerate(
                    (
                        (res[(0, *at)], ta[at] - cl[at]),
                        (res[(3, *at)], td[at] - cr[at]),
                        (q0[at] - alpha * t2[(1, *at)], -ca[at]),
                    )
                ):
                    rest = q - image
                    parts[n][0] = parts[n][0] + rest * rest
                    parts[n][1] = parts[n][1] + rest * image
                    parts[n][2] = parts[n][2] + image * image
            adds = [between] + [a + inside * b + begin * c for a, b, c in zip(*parts)]
            mask = owned(k, colour)
            return tuple(a + jnp.where(mask, b, 0.0) for a, b in zip(carry, adds))

        between, *squares = lax.fori_loop(0, K, body, (zero,) * 4)
        rows[0].append(sums[0])
        rows[1].append(sums[1] - between)
        for i in range(3):
            rows[2 + i].append(sums[2 + i] + squares[i])
    out[...] = rows_of([value for row in rows for value in row], 16)


def join_second(where, table, arrays):
    return pl.pallas_call(
        join_second_kernel,
        out_shape=jax.ShapeDtypeStruct((16, LANES), jnp.float32),
        in_specs=[SM] + [VM] * (1 + 10 * NRHS),
        out_specs=VM,
        compiler_params=pltpu.CompilerParams(vmem_limit_bytes=VMEM_LIMIT),
        cost_estimate=estimate(40, 2),
    )(where, table, *arrays)


def last_kernel(where, table, after, *refs):
    norms, mine_u, mine_q, held, sems = refs[-5:]
    colour = where[0]
    low = pl.multiple_of(colour * (WIN - OWN), 8)
    rows = []
    pending = []
    for r in range(NRHS):
        q0, t2, c, c3, res, c0l, ca, cm, t0l, ta, tm = refs[11 * r : 11 * r + 11]
        first = ratio(table, r, NRHS + r)
        second = ratio(after, r, NRHS + r)
        more = second - 1.0
        square, cross, own = (
            jnp.sum(after[i * NRHS + r : i * NRHS + r + 1, :], axis=1, keepdims=True) for i in (2, 3, 4)
        )
        total = square - 2.0 * more * cross + more * more * own
        rows.append(jnp.broadcast_to(jnp.sqrt(jnp.maximum(total, 0.0)), (1, LANES)))
        one = jnp.broadcast_to(first, (8, LANES))
        two = jnp.broadcast_to(second, (8, LANES))
        slot = r % 2
        if r >= 2:
            for copy in pending[r - 2]:
                copy.wait()

        def body(k, _, q0=q0, t2=t2, c=c, c3=c3, res=res, c0l=c0l, ca=ca, cm=cm, t0l=t0l, ta=ta, tm=tm, one=one, two=two, slot=slot):
            for t in range(TILES):
                at = (k, slice(None), tile(t))
                firsts = [c[(0, *at)], c[(1, *at)], c[(2, *at)], c3[at]]
                seconds = [c0l[at], ca[at], cm[(0, *at)], cm[(1, *at)]]
                residuals = [q0[at] - one * t2[(1, *at)], res[(0, *at)], res[(1, *at)], res[(2, *at)]]
                images = [t0l[at] - ca[at], ta[at] - c0l[at], tm[(0, *at)], tm[(1, *at)]]
                for p in range(4):
                    rows_at = pl.ds(k, 8, stride=K)
                    held[slot, 0, p, t, rows_at, :] = one * firsts[p] + two * seconds[p]
                    held[slot, 1, p, t, rows_at, :] = residuals[p] - two * images[p]
            return 0

        lax.fori_loop(0, K, body, 0)
        copies = []
        for n, out in enumerate((mine_u, mine_q)):
            for t in range(TILES):
                copies.append(
                    pltpu.make_async_copy(
                        held.at[slot, n, :, t, pl.ds(low, OWN), :],
                        out.at[t // (TILES // 2), r, :, :, tile(t % (TILES // 2))],
                        sems.at[slot, n, t],
                    )
                )
        for copy in copies:
            copy.start()
        pending.append(copies)
    for copies in pending[max(0, NRHS - 2) :]:
        for copy in copies:
            copy.wait()
    rows += [jnp.zeros((1, LANES), jnp.float32)] * (8 - NRHS)
    norms[...] = jnp.concatenate(rows, axis=0)


def last(where, table, after, arrays):
    halves = jax.ShapeDtypeStruct((2, NRHS, 4, OWN, NZ // 2), jnp.float32)
    return pl.pallas_call(
        last_kernel,
        out_shape=[jax.ShapeDtypeStruct((8, LANES), jnp.float32), halves, halves],
        in_specs=[SM] + [VM] * (2 + 11 * NRHS),
        out_specs=[VM, pl.BlockSpec(memory_space=pl.ANY), pl.BlockSpec(memory_space=pl.ANY)],
        scratch_shapes=[
            pltpu.VMEM((2, 2, 4, TILES, WIN, LANES), jnp.float32),
            pltpu.SemaphoreType.DMA((2, 2, TILES)),
        ],
        compiler_params=pltpu.CompilerParams(vmem_limit_bytes=40 * 1024 * 1024),
        cost_estimate=estimate(70, 3),
    )(where, table, after, *arrays)


def everywhere(value):
    value = value + lax.ppermute(value, "colour", [(0, 1), (1, 0)])
    for axis in reversed(SUB):
        count = lax.axis_size(axis)
        a, b, c = (
            lax.ppermute(value, axis, [(i, i ^ mask) for i in range(count)]) for mask in (1, 2, 3)
        )
        value = (value + a) + (b + c)
    return value


def shards(rhs, diagonal):
    colour = lax.axis_index("colour")
    device = lax.axis_index(SUB)
    total = lax.axis_size(SUB)
    forward = [(i, i + 1) for i in range(total - 1)]
    backward = [(i + 1, i) for i in range(total - 1)]
    where = jnp.stack([colour, device, jnp.int32(total)]).astype(jnp.int32)

    def right(value):
        return lax.ppermute(value, SUB, forward)

    def left(value):
        return lax.ppermute(value, SUB, backward)

    *q0, d0 = (outer := prepare((0, 3), where, rhs, diagonal))[: NRHS + 1]
    *q3, d3 = outer[NRHS + 1 :]
    dh = right(d3)
    qh = [right(q) for q in q3]
    d4 = left(d0)
    q4 = [left(q) for q in q0]
    *q1, d1 = (inner := prepare((1, 2), where, rhs, diagonal))[: NRHS + 1]
    *q2, d2 = inner[NRHS + 1 :]

    firsts = [
        first_solve(where, qh[r], q0[r], q1[r], q2[r], dh, d0, d1, d2) for r in range(NRHS)
    ]
    ch, c, t2, t12, sums = zip(*firsts)
    cr = [left(v) for v in ch]
    tr = [left(v) for v in t2]
    table = everywhere(join(where, c, cr, sums))
    seconds = [
        second_solve(
            r, where, table, q1[r], q2[r], q3[r], q4[r], d1, d2, d3, d4, c[r], cr[r], tr[r], t12[r]
        )
        for r in range(NRHS)
    ]
    ca, cm, cd, ta, tm, td, res, sums = zip(*seconds)
    cl = [right(v) for v in cd]
    cr1 = [left(v) for v in ca]
    tl = [right(v) for v in td]
    arrays = [
        a
        for r in range(NRHS)
        for a in (res[r], ca[r], cd[r], ta[r], td[r], cl[r], cr1[r], q0[r], t2[r], sums[r])
    ]
    after = everywhere(join_second(where, table, arrays))
    arrays = [
        a
        for r in range(NRHS)
        for a in (q0[r], t2[r], c[r], cr[r], res[r], cl[r], ca[r], cm[r], tl[r], ta[r], tm[r])
    ]
    norms, us, qs = last(where, table, after, arrays)

    def whole(halves):
        mine = lax.dynamic_index_in_dim(halves, colour, 0, keepdims=False)
        other = lax.dynamic_index_in_dim(halves, 1 - colour, 0, keepdims=False)
        other = lax.ppermute(other, "colour", [(0, 1), (1, 0)])
        first = jnp.where(colour == 0, mine, other)
        second = jnp.where(colour == 0, other, mine)
        return jnp.concatenate([first, second], axis=2)

    return whole(us), whole(qs), norms[:NRHS, 0]


def solution(mesh):
    torus = Mesh(
        mesh.devices.reshape(mesh.shape["colour"], 4, 4, 4), ("colour", "sub_0", "sub_1", "sub_2")
    )
    return jax.shard_map(
        shards,
        mesh=torus,
        in_specs=(P(None, SUB, None, None), P(SUB, None, None)),
        out_specs=(P(None, SUB, None, "colour"), P(None, SUB, None, "colour"), P()),
        check_vma=False,
    )
```

```python
import functools

import jax
import jax.numpy as jnp
from jax import lax
from jax.experimental import pallas as pl
from jax.experimental.pallas import tpu as pltpu
from jax.sharding import Mesh
from jax.sharding import PartitionSpec as P

OMEGA = 0.8
SWEEPS = 8
NY = 256
NZ = 512
NRHS = 3
OWN = 128
WIN = 144
K = WIN // 8
LANES = 128
TILES = NZ // LANES
SUB = ("sub_0", "sub_1", "sub_2")
VMEM_LIMIT = 12 * 1024 * 1024


def powers():
    total = [0.0] * SWEEPS
    power = [1.0]
    for _ in range(SWEEPS):
        for i, value in enumerate(power):
            total[i] += value
        longer = [0.0] * (len(power) + 1)
        for i, value in enumerate(power):
            longer[i] += (1.0 - OMEGA) * value
            longer[i + 1] += value
        power = longer
    return total


COEFFICIENTS = powers()
PLANE = (K, 8, NZ)
VM = pl.BlockSpec(memory_space=pltpu.VMEM)
SM = pl.BlockSpec(memory_space=pltpu.SMEM)
ANY = pl.BlockSpec(memory_space=pl.ANY)
HBM = pl.BlockSpec(memory_space=pltpu.MemorySpace.HBM)


def shape_of(*lead):
    return jax.ShapeDtypeStruct((*lead, *PLANE), jnp.float32)


def tile(t):
    return slice(t * LANES, (t + 1) * LANES)


def lanes():
    return lax.broadcasted_iota(jnp.int32, (8, LANES), 1)


def sublanes():
    return lax.broadcasted_iota(jnp.int32, (8, LANES), 0)


def owned(k, colour):
    row = sublanes() * K + k - colour * (WIN - OWN)
    return (row >= 0) & (row < OWN)


def close_edges(buf):
    sub = sublanes()
    for p in range(4):
        for t in range(TILES):
            last = pltpu.roll(buf[p, K, :, tile(t)], 1, 0)
            buf[p, 0, :, tile(t)] = jnp.where(sub == 0, 0.0, last)
            first = pltpu.roll(buf[p, 1, :, tile(t)], 7, 0)
            buf[p, K + 1, :, tile(t)] = jnp.where(sub == 7, 0.0, first)


def beside(buf, k):
    lane = lanes()
    first, last = lane == 0, lane == LANES - 1
    here = [[buf[p, k + 1, :, tile(t)] for t in range(TILES)] for p in range(4)]
    sums = []
    for p in range(4):
        up = [pltpu.roll(v, 1, 1) for v in here[p]]
        down = [pltpu.roll(v, LANES - 1, 1) for v in here[p]]
        row = []
        for t in range(TILES):
            total = jnp.where(first, up[t - 1] if t else 0.0, up[t])
            total = total + jnp.where(last, down[t + 1] if t + 1 < TILES else 0.0, down[t])
            total = total + (buf[p, k, :, tile(t)] + buf[p, k + 2, :, tile(t)])
            if p == 0:
                total = total + here[1][t]
            elif p == 3:
                total = total + here[2][t]
            else:
                total = total + (here[p - 1][t] + here[p + 1][t])
            row.append(total)
        sums.append(row)
    return sums, here


def solve(source, scale, one, two):
    close_edges(one)
    bufs = (one, two)
    for step, power in enumerate(range(SWEEPS - 2, -1, -1)):
        src, dst = bufs[step % 2], bufs[1 - step % 2]
        factor = COEFFICIENTS[power]

        def body(k, _, src=src, dst=dst, factor=factor):
            sums, _ = beside(src, k)
            for p in range(4):
                for t in range(TILES):
                    dst[p, k + 1, :, tile(t)] = (
                        scale[p, k, :, tile(t)] * sums[p][t]
                        + factor * source[p, k, :, tile(t)]
                    )
            return 0

        lax.fori_loop(0, K, body, 0, unroll=True)
        close_edges(dst)
    return bufs[(SWEEPS - 1) % 2]


def prepare_kernel(packs, where, rhs, diag, *refs):
    outs, (held, sem) = refs[: len(packs)], refs[len(packs) :]
    low = pl.multiple_of(where[0] * (NY - WIN), 8)
    places = [(out, i, *item) for out, pack in zip(outs, packs) for i, item in enumerate(pack)]
    copies = []
    for n, (_, _, plane, r) in enumerate(places):
        for t in range(TILES):
            if r < NRHS:
                src = rhs.at[r, plane, pl.ds(low, WIN), tile(t)]
            else:
                src = diag.at[plane, pl.ds(low, WIN), tile(t)]
            copies.append(pltpu.make_async_copy(src, held.at[n, t], sem.at[n, t]))
    for copy in copies:
        copy.start()
    for n, (out, i, _, _) in enumerate(places):
        for t in range(TILES):
            copies[n * TILES + t].wait()
            for k in range(K):
                out[i, k, :, tile(t)] = held[n, t, pl.ds(k, 8, stride=K), :]


def prepare(packs, where, rhs, diag):
    count = sum(len(pack) for pack in packs)
    return pl.pallas_call(
        functools.partial(prepare_kernel, packs),
        out_shape=[shape_of(len(pack)) for pack in packs],
        in_specs=[SM, HBM, HBM],
        out_specs=[VM] * len(packs),
        scratch_shapes=[
            pltpu.VMEM((count, TILES, WIN, LANES), jnp.float32),
            pltpu.SemaphoreType.DMA((count, TILES)),
        ],
        compiler_params=pltpu.CompilerParams(vmem_limit_bytes=VMEM_LIMIT),
        cost_estimate=pl.CostEstimate(flops=0, bytes_accessed=count * 600000, transcendentals=0),
    )(where, *(pltpu.with_memory_space_constraint(v, pltpu.MemorySpace.HBM) for v in (rhs, diag)))


def local(buf, diags, k):
    sums, here = beside(buf, k)
    images = [
        [(6.0 + diags[p][k, :, tile(t)]) * here[p][t] - sums[p][t] for t in range(TILES)]
        for p in range(4)
    ]
    return images, here


def fill(k, p, q, d, keep, scale, source, one):
    for t in range(TILES):
        s = OMEGA / (6.0 + d[k, :, tile(t)])
        if keep is not None:
            s = s * keep
        g = s * q[t]
        scale[p, k, :, tile(t)] = s
        source[p, k, :, tile(t)] = g
        one[p, k + 1, :, tile(t)] = g


SCRATCH = [
    pltpu.VMEM((4, K, 8, NZ), jnp.float32),
    pltpu.VMEM((4, K, 8, NZ), jnp.float32),
    pltpu.VMEM((4, K + 2, 8, NZ), jnp.float32),
    pltpu.VMEM((4, K + 2, 8, NZ), jnp.float32),
]


def halo(r):
    return (0, 1) if r == 0 else (1, r - 1)


def first_kernel(r, where, pd, ph, p0, p1, p2, ch, c, t2, t12, sums, scale, source, one, two):
    colour, device = where[0], where[1]
    keep = (device > 0).astype(jnp.float32)
    which, at = halo(r)
    qs = ((pd, ph)[which].at[at], p0.at[r], p1.at[r], p2.at[r])
    ds = (pd.at[0], p0.at[NRHS], p1.at[NRHS], p2.at[NRHS])

    def start(k, _):
        for p in range(4):
            q = [qs[p][k, :, tile(t)] for t in range(TILES)]
            fill(k, p, q, ds[p], keep if p == 0 else None, scale, source, one)
        return 0

    lax.fori_loop(0, K, start, 0, unroll=True)
    found = solve(source, scale, one, two)

    def finish(k, carry):
        upper, lower = carry
        images, here = local(found, ds, k)
        mask = owned(k, colour)
        up, low = 0.0, 0.0
        for p in range(4):
            for t in range(TILES):
                value = here[p][t]
                up = up + qs[p][k, :, tile(t)] * value
                low = low + images[p][t] * value
                if p == 0:
                    ch[k, :, tile(t)] = value
                else:
                    c[p - 1, k, :, tile(t)] = value
                if p < 2:
                    t2[p, k, :, tile(t)] = images[p][t]
                else:
                    t12[p - 2, k, :, tile(t)] = images[p][t]
        return upper + jnp.where(mask, up, 0.0), lower + jnp.where(mask, low, 0.0)

    zero = jnp.zeros((8, LANES), jnp.float32)
    upper, lower = lax.fori_loop(0, K, finish, (zero, zero), unroll=True)
    sums[0] = upper
    sums[1] = lower


def estimate(planes, passes):
    return pl.CostEstimate(
        flops=passes * 4 * K * 8 * NZ * 10, bytes_accessed=planes * K * 8 * NZ * 4, transcendentals=0
    )


def first_solve(r, where, *arrays):
    return pl.pallas_call(
        functools.partial(first_kernel, r),
        out_shape=[
            shape_of(),
            shape_of(3),
            shape_of(2),
            shape_of(2),
            jax.ShapeDtypeStruct((2, 8, LANES), jnp.float32),
        ],
        in_specs=[SM] + [VM] * 5,
        out_specs=[VM] * 5,
        scratch_shapes=SCRATCH,
        compiler_params=pltpu.CompilerParams(vmem_limit_bytes=VMEM_LIMIT),
        cost_estimate=estimate(16, SWEEPS + 1),
    )(where, *arrays)


def rows_of(values, count):
    rows = [jnp.sum(v, axis=0, keepdims=True) for v in values]
    rows += [jnp.zeros((1, LANES), jnp.float32)] * (count - len(rows))
    return jnp.concatenate(rows, axis=0)


def join_kernel(where, *refs):
    cs, rights, sums, out = refs[:NRHS], refs[NRHS : 2 * NRHS], refs[2 * NRHS : 3 * NRHS], refs[-1]
    colour = where[0]
    zero = jnp.zeros((8, LANES), jnp.float32)
    uppers, lowers = [], []
    for r in range(NRHS):

        def body(k, total, r=r):
            add = 0.0
            for t in range(TILES):
                add = add + cs[r][2, k, :, tile(t)] * rights[r][k, :, tile(t)]
            return total + jnp.where(owned(k, colour), add, 0.0)

        between = lax.fori_loop(0, K, body, zero, unroll=6)
        uppers.append(sums[r][0])
        lowers.append(sums[r][1] - 2.0 * between)
    out[...] = rows_of(uppers + lowers, 8)


def join(where, cs, rights, sums):
    return pl.pallas_call(
        join_kernel,
        out_shape=jax.ShapeDtypeStruct((8, LANES), jnp.float32),
        in_specs=[SM] + [VM] * (3 * NRHS),
        out_specs=VM,
        compiler_params=pltpu.CompilerParams(vmem_limit_bytes=VMEM_LIMIT),
        cost_estimate=estimate(12, 1),
    )(where, *cs, *rights, *sums)


def ratio(table, upper, lower):
    top = jnp.sum(table[upper : upper + 1, :], axis=1, keepdims=True)
    bottom = jnp.sum(table[lower : lower + 1, :], axis=1, keepdims=True)
    return top / bottom


def second_kernel(
    r, where, table, p1, p2, pd, ph, p4, c, cr, tr, t12,
    ca, cm, cd, ta, tm, td, res, sums, scale, source, one, two,
):
    colour, device, count = where[0], where[1], where[2]
    keep = (device < count - 1).astype(jnp.float32)
    alpha = jnp.broadcast_to(ratio(table, r, NRHS + r), (8, LANES))
    which, place_at = halo(r)
    q1, q2, q3, q4 = p1.at[r], p2.at[r], (pd, ph)[which].at[place_at], p4.at[r]
    ds = (p1.at[NRHS], p2.at[NRHS], pd.at[0], p4.at[NRHS])

    def start(k, _):
        for p in range(4):
            values = []
            for t in range(TILES):
                if p == 0:
                    image = t12[0, k, :, tile(t)]
                    q = q1[k, :, tile(t)]
                elif p == 1:
                    image = t12[1, k, :, tile(t)] - cr[k, :, tile(t)]
                    q = q2[k, :, tile(t)]
                elif p == 2:
                    image = tr[0, k, :, tile(t)] - c[2, k, :, tile(t)]
                    q = q3[k, :, tile(t)]
                else:
                    image = tr[1, k, :, tile(t)]
                    q = q4[k, :, tile(t)]
                value = q - alpha * image
                res[p, k, :, tile(t)] = value
                values.append(value)
            fill(k, p, values, ds[p], keep if p == 3 else None, scale, source, one)
        return 0

    lax.fori_loop(0, K, start, 0, unroll=True)
    found = solve(source, scale, one, two)

    def finish(k, carry):
        images, here = local(found, ds, k)
        mask = owned(k, colour)
        adds = [0.0] * 5
        for p in range(4):
            for t in range(TILES):
                value, image, q = here[p][t], images[p][t], res[p, k, :, tile(t)]
                adds[0] = adds[0] + q * value
                adds[1] = adds[1] + image * value
                if p in (1, 2):
                    rest = q - image
                    adds[2] = adds[2] + rest * rest
                    adds[3] = adds[3] + rest * image
                    adds[4] = adds[4] + image * image
                    cm[p - 1, k, :, tile(t)] = value
                    tm[p - 1, k, :, tile(t)] = image
                else:
                    (ca if p == 0 else cd)[k, :, tile(t)] = value
                    (ta if p == 0 else td)[k, :, tile(t)] = image
        return tuple(a + jnp.where(mask, b, 0.0) for a, b in zip(carry, adds))

    zero = jnp.zeros((8, LANES), jnp.float32)
    found_sums = lax.fori_loop(0, K, finish, (zero,) * 5, unroll=True)
    for i in range(5):
        sums[i] = found_sums[i]


def second_solve(r, where, table, *arrays):
    return pl.pallas_call(
        functools.partial(second_kernel, r),
        out_shape=[
            shape_of(),
            shape_of(2),
            shape_of(),
            shape_of(),
            shape_of(2),
            shape_of(),
            shape_of(4),
            jax.ShapeDtypeStruct((5, 8, LANES), jnp.float32),
        ],
        in_specs=[SM] + [VM] * 10,
        out_specs=[VM] * 8,
        scratch_shapes=SCRATCH,
        compiler_params=pltpu.CompilerParams(vmem_limit_bytes=VMEM_LIMIT),
        cost_estimate=estimate(28, SWEEPS + 1),
    )(where, table, *arrays)


def join_second_kernel(where, table, *refs):
    out = refs[-1]
    colour, device, count = where[0], where[1], where[2]
    begin = (device == 0).astype(jnp.float32)
    inside = (device < count - 1).astype(jnp.float32)
    zero = jnp.zeros((8, LANES), jnp.float32)
    rows = [[] for _ in range(5)]
    for r in range(NRHS):
        res, ca, cd, ta, td, cl, cr, t2, sums = refs[1 + 9 * r : 10 + 9 * r]
        q0 = refs[0].at[r]
        alpha = jnp.broadcast_to(ratio(table, r, NRHS + r), (8, LANES))

        def body(k, carry, res=res, ca=ca, cd=cd, ta=ta, td=td, cl=cl, cr=cr, q0=q0, t2=t2, alpha=alpha):
            between = 0.0
            parts = [[0.0] * 3 for _ in range(3)]
            for t in range(TILES):
                at = (k, slice(None), tile(t))
                between = between + ca[at] * cl[at] + cd[at] * cr[at]
                for n, (q, image) in enumerate(
                    (
                        (res[(0, *at)], ta[at] - cl[at]),
                        (res[(3, *at)], td[at] - cr[at]),
                        (q0[at] - alpha * t2[(1, *at)], -ca[at]),
                    )
                ):
                    rest = q - image
                    parts[n][0] = parts[n][0] + rest * rest
                    parts[n][1] = parts[n][1] + rest * image
                    parts[n][2] = parts[n][2] + image * image
            adds = [between] + [a + inside * b + begin * c for a, b, c in zip(*parts)]
            mask = owned(k, colour)
            return tuple(a + jnp.where(mask, b, 0.0) for a, b in zip(carry, adds))

        between, *squares = lax.fori_loop(0, K, body, (zero,) * 4, unroll=6)
        rows[0].append(sums[0])
        rows[1].append(sums[1] - between)
        for i in range(3):
            rows[2 + i].append(sums[2 + i] + squares[i])
    out[...] = rows_of([value for row in rows for value in row], 16)


def join_second(where, table, arrays):
    return pl.pallas_call(
        join_second_kernel,
        out_shape=jax.ShapeDtypeStruct((16, LANES), jnp.float32),
        in_specs=[SM] + [VM] * (2 + 9 * NRHS),
        out_specs=VM,
        compiler_params=pltpu.CompilerParams(vmem_limit_bytes=VMEM_LIMIT),
        cost_estimate=estimate(40, 2),
    )(where, table, *arrays)


def last_kernel(where, table, after, *refs):
    norms, full_u, full_q, send_u, send_q, held, sems = refs[-7:]
    colour = where[0]
    low = pl.multiple_of(colour * (WIN - OWN), 8)
    start = pl.multiple_of(colour * OWN, 8)
    rows = []
    pending = []
    for r in range(NRHS):
        t2, c, c3, res, c0l, ca, cm, t0l, ta, tm = refs[1 + 10 * r : 11 + 10 * r]
        q0 = refs[0].at[r]
        first = ratio(table, r, NRHS + r)
        second = ratio(after, r, NRHS + r)
        more = second - 1.0
        square, cross, own = (
            jnp.sum(after[i * NRHS + r : i * NRHS + r + 1, :], axis=1, keepdims=True) for i in (2, 3, 4)
        )
        total = square - 2.0 * more * cross + more * more * own
        rows.append(jnp.broadcast_to(jnp.sqrt(jnp.maximum(total, 0.0)), (1, LANES)))
        one = jnp.broadcast_to(first, (8, LANES))
        two = jnp.broadcast_to(second, (8, LANES))
        slot = r % 2
        if r >= 2:
            for copy in pending[r - 2]:
                copy.wait()

        def body(k, _, q0=q0, t2=t2, c=c, c3=c3, res=res, c0l=c0l, ca=ca, cm=cm, t0l=t0l, ta=ta, tm=tm, one=one, two=two, slot=slot):
            for t in range(TILES):
                at = (k, slice(None), tile(t))
                firsts = [c[(0, *at)], c[(1, *at)], c[(2, *at)], c3[at]]
                seconds = [c0l[at], ca[at], cm[(0, *at)], cm[(1, *at)]]
                residuals = [q0[at] - one * t2[(1, *at)], res[(0, *at)], res[(1, *at)], res[(2, *at)]]
                images = [t0l[at] - ca[at], ta[at] - c0l[at], tm[(0, *at)], tm[(1, *at)]]
                for p in range(4):
                    rows_at = pl.ds(k, 8, stride=K)
                    held[slot, 0, p, t, rows_at, :] = one * firsts[p] + two * seconds[p]
                    held[slot, 1, p, t, rows_at, :] = residuals[p] - two * images[p]
            return 0

        lax.fori_loop(0, K, body, 0, unroll=6)
        copies = []
        half = TILES // 2
        for n, (full, send) in enumerate(((full_u, send_u), (full_q, send_q))):
            for t in range(half):
                copies.append(
                    pltpu.make_async_copy(
                        held.at[slot, n, :, colour * half + t, pl.ds(low, OWN), :],
                        full.at[r, :, pl.ds(start, OWN), tile(t)],
                        sems.at[slot, n, t],
                    )
                )
                copies.append(
                    pltpu.make_async_copy(
                        held.at[slot, n, :, (1 - colour) * half + t, pl.ds(low, OWN), :],
                        send.at[r, :, :, tile(t)],
                        sems.at[slot, n, half + t],
                    )
                )
        for copy in copies:
            copy.start()
        pending.append(copies)
    for copies in pending[max(0, NRHS - 2) :]:
        for copy in copies:
            copy.wait()
    rows += [jnp.zeros((1, LANES), jnp.float32)] * (8 - NRHS)
    norms[...] = jnp.concatenate(rows, axis=0)


def last(where, table, after, arrays):
    full = jax.ShapeDtypeStruct((NRHS, 4, NY, NZ // 2), jnp.float32)
    send = jax.ShapeDtypeStruct((NRHS, 4, OWN, NZ // 2), jnp.float32)
    return pl.pallas_call(
        last_kernel,
        out_shape=[jax.ShapeDtypeStruct((8, LANES), jnp.float32), full, full, send, send],
        in_specs=[SM] + [VM] * (3 + 10 * NRHS),
        out_specs=[VM, HBM, HBM, ANY, ANY],
        scratch_shapes=[
            pltpu.VMEM((2, 2, 4, TILES, WIN, LANES), jnp.float32),
            pltpu.SemaphoreType.DMA((2, 2, TILES)),
        ],
        compiler_params=pltpu.CompilerParams(vmem_limit_bytes=VMEM_LIMIT),
        cost_estimate=estimate(70, 3),
    )(where, table, after, *arrays)


def place_kernel(where, got_u, got_q, in_u, in_q, full_u, full_q, sems):
    start = pl.multiple_of((1 - where[0]) * OWN, 8)
    copies = []
    for n, (got, full) in enumerate(((got_u, full_u), (got_q, full_q))):
        for r in range(NRHS):
            for p in range(4):
                copies.append(
                    pltpu.make_async_copy(
                        got.at[r, p], full.at[r, p, pl.ds(start, OWN)], sems.at[n, r, p]
                    )
                )
    for copy in copies:
        copy.start()
    for copy in copies:
        copy.wait()


def place(where, got_u, got_q, full_u, full_q):
    full = jax.ShapeDtypeStruct((NRHS, 4, NY, NZ // 2), jnp.float32)
    return pl.pallas_call(
        place_kernel,
        out_shape=[full, full],
        in_specs=[SM] + [VM] * 2 + [HBM] * 2,
        out_specs=[HBM] * 2,
        scratch_shapes=[pltpu.SemaphoreType.DMA((2, NRHS, 4))],
        input_output_aliases={3: 0, 4: 1},
        compiler_params=pltpu.CompilerParams(vmem_limit_bytes=4 * 1024 * 1024),
    )(where, got_u, got_q, full_u, full_q)


def everywhere(value, after_first=()):
    for axis in (*reversed(SUB), "colour"):
        count = lax.axis_size(axis)
        others = [
            lax.ppermute(value, axis, [(i, i ^ mask) for i in range(count)])
            for mask in range(1, count)
        ]
        if count == 2:
            value = value + others[0]
        else:
            value = (value + others[0]) + (others[1] + others[2])
        if axis == SUB[-1] and after_first:
            value, after_first = lax.optimization_barrier((value, after_first))
    return value, after_first


def shards(rhs, diagonal):
    colour = lax.axis_index("colour")
    device = lax.axis_index(SUB)
    total = lax.axis_size(SUB)
    forward = [(i, i + 1) for i in range(total - 1)]
    backward = [(i + 1, i) for i in range(total - 1)]
    where = jnp.stack([colour, device, jnp.int32(total)]).astype(jnp.int32)

    def right(value):
        return lax.ppermute(value, SUB, forward)

    def left(value):
        return lax.ppermute(value, SUB, backward)

    everything = range(NRHS + 1)
    pd, ph, p0 = prepare(
        (((3, NRHS), (3, 0)), tuple((3, r) for r in range(1, NRHS)), tuple((0, r) for r in everything)),
        where, rhs, diagonal,
    )
    hd, hh = right(pd), right(ph)
    p4 = left(p0)
    p1, p2 = prepare(tuple(tuple((plane, r) for r in everything) for plane in (1, 2)), where, rhs, diagonal)

    firsts = [first_solve(0, where, hd, hh, p0, p1, p2)]
    hd, p4 = lax.optimization_barrier((hd, p4))
    firsts += [first_solve(r, where, hd, hh, p0, p1, p2) for r in range(1, NRHS)]
    ch, c, t2, t12, sums = zip(*firsts)
    cr = [left(v) for v in ch]
    tr = [left(t2[0])]
    table, late = everywhere(join(where, c, cr, sums), tuple(t2[1:]))
    tr += [left(v) for v in late]
    seconds = [
        second_solve(
            r, where, table, p1, p2, pd, ph, p4, c[r], cr[r], tr[r], t12[r]
        )
        for r in range(NRHS)
    ]
    ca, cm, cd, ta, tm, td, res, sums = zip(*seconds)
    cl = [right(v) for v in cd]
    cr1 = [left(v) for v in ca]
    tl = [right(td[0])]
    arrays = [
        a
        for r in range(NRHS)
        for a in (res[r], ca[r], cd[r], ta[r], td[r], cl[r], cr1[r], t2[r], sums[r])
    ]
    after, late = everywhere(join_second(where, table, [p0, *arrays]), tuple(td[1:]))
    tl += [right(v) for v in late]
    arrays = [
        a
        for r in range(NRHS)
        for a in (t2[r], c[r], cr[r], res[r], cl[r], ca[r], cm[r], tl[r], ta[r], tm[r])
    ]
    norms, full_u, full_q, send_u, send_q = last(where, table, after, [p0, *arrays])
    pairs = [(0, 1), (1, 0)]
    got_u, got_q = (lax.ppermute(v, "colour", pairs) for v in (send_u, send_q))
    full_u, full_q = place(where, got_u, got_q, full_u, full_q)
    return full_u, full_q, norms[:NRHS, 0]


def solution(mesh):
    torus = Mesh(
        mesh.devices.reshape(mesh.shape["colour"], 4, 4, 4), ("colour", "sub_0", "sub_1", "sub_2")
    )
    return jax.shard_map(
        shards,
        mesh=torus,
        in_specs=(P(None, SUB, None, None), P(SUB, None, None)),
        out_specs=(P(None, SUB, None, "colour"), P(None, SUB, None, "colour"), P()),
        check_vma=False,
    )
```

```python
import functools

import jax
import jax.numpy as jnp
from jax import lax
from jax.experimental import pallas as pl
from jax.experimental.pallas import tpu as pltpu
from jax.sharding import Mesh
from jax.sharding import PartitionSpec as P

OMEGA = 0.8
SWEEPS = 8
NY = 256
NZ = 512
NRHS = 3
OWN = 128
WIN = 144
K = WIN // 8
LANES = 128
TILES = NZ // LANES
SUB = ("sub_0", "sub_1", "sub_2")
VMEM_LIMIT = 12 * 1024 * 1024


def powers():
    total = [0.0] * SWEEPS
    power = [1.0]
    for _ in range(SWEEPS):
        for i, value in enumerate(power):
            total[i] += value
        longer = [0.0] * (len(power) + 1)
        for i, value in enumerate(power):
            longer[i] += (1.0 - OMEGA) * value
            longer[i + 1] += value
        power = longer
    return total


COEFFICIENTS = powers()
PLANE = (K, 8, NZ)
VM = pl.BlockSpec(memory_space=pltpu.VMEM)
SM = pl.BlockSpec(memory_space=pltpu.SMEM)
ANY = pl.BlockSpec(memory_space=pl.ANY)
HBM = pl.BlockSpec(memory_space=pltpu.MemorySpace.HBM)


def shape_of(*lead):
    return jax.ShapeDtypeStruct((*lead, *PLANE), jnp.float32)


def tile(t):
    return slice(t * LANES, (t + 1) * LANES)


def lanes():
    return lax.broadcasted_iota(jnp.int32, (8, LANES), 1)


def sublanes():
    return lax.broadcasted_iota(jnp.int32, (8, LANES), 0)


def owned(k, colour):
    row = sublanes() * K + k - colour * (WIN - OWN)
    return (row >= 0) & (row < OWN)


def close_edges(buf):
    sub = sublanes()
    for p in range(4):
        for t in range(TILES):
            last = pltpu.roll(buf[p, K, :, tile(t)], 1, 0)
            buf[p, 0, :, tile(t)] = jnp.where(sub == 0, 0.0, last)
            first = pltpu.roll(buf[p, 1, :, tile(t)], 7, 0)
            buf[p, K + 1, :, tile(t)] = jnp.where(sub == 7, 0.0, first)


def beside(buf, k):
    lane = lanes()
    first, last = lane == 0, lane == LANES - 1
    here = [[buf[p, k + 1, :, tile(t)] for t in range(TILES)] for p in range(4)]
    sums = []
    for p in range(4):
        up = [pltpu.roll(v, 1, 1) for v in here[p]]
        down = [pltpu.roll(v, LANES - 1, 1) for v in here[p]]
        row = []
        for t in range(TILES):
            total = jnp.where(first, up[t - 1] if t else 0.0, up[t])
            total = total + jnp.where(last, down[t + 1] if t + 1 < TILES else 0.0, down[t])
            total = total + (buf[p, k, :, tile(t)] + buf[p, k + 2, :, tile(t)])
            if p == 0:
                total = total + here[1][t]
            elif p == 3:
                total = total + here[2][t]
            else:
                total = total + (here[p - 1][t] + here[p + 1][t])
            row.append(total)
        sums.append(row)
    return sums, here


def solve(source, scale, one, two):
    close_edges(one)
    bufs = (one, two)
    for step, power in enumerate(range(SWEEPS - 2, -1, -1)):
        src, dst = bufs[step % 2], bufs[1 - step % 2]
        factor = COEFFICIENTS[power]

        def body(k, _, src=src, dst=dst, factor=factor):
            sums, _ = beside(src, k)
            for p in range(4):
                for t in range(TILES):
                    dst[p, k + 1, :, tile(t)] = (
                        scale[p, k, :, tile(t)] * sums[p][t]
                        + factor * source[p, k, :, tile(t)]
                    )
            return 0

        lax.fori_loop(0, K, body, 0, unroll=True)
        close_edges(dst)
    return bufs[(SWEEPS - 1) % 2]


def prepare_kernel(packs, where, rhs, diag, *refs):
    outs, (held, sem) = refs[: len(packs)], refs[len(packs) :]
    low = pl.multiple_of(where[0] * (NY - WIN), 8)
    places = [(out, i, *item) for out, pack in zip(outs, packs) for i, item in enumerate(pack)]
    copies = []
    for n, (_, _, plane, r) in enumerate(places):
        for t in range(TILES):
            if r < NRHS:
                src = rhs.at[r, plane, pl.ds(low, WIN), tile(t)]
            else:
                src = diag.at[plane, pl.ds(low, WIN), tile(t)]
            copies.append(pltpu.make_async_copy(src, held.at[n, t], sem.at[n, t]))
    for copy in copies:
        copy.start()
    for n, (out, i, _, _) in enumerate(places):
        for t in range(TILES):
            copies[n * TILES + t].wait()
            for k in range(K):
                out[i, k, :, tile(t)] = held[n, t, pl.ds(k, 8, stride=K), :]


def prepare(packs, where, rhs, diag):
    count = sum(len(pack) for pack in packs)
    return pl.pallas_call(
        functools.partial(prepare_kernel, packs),
        out_shape=[shape_of(len(pack)) for pack in packs],
        in_specs=[SM, HBM, HBM],
        out_specs=[VM] * len(packs),
        scratch_shapes=[
            pltpu.VMEM((count, TILES, WIN, LANES), jnp.float32),
            pltpu.SemaphoreType.DMA((count, TILES)),
        ],
        compiler_params=pltpu.CompilerParams(vmem_limit_bytes=VMEM_LIMIT),
        cost_estimate=pl.CostEstimate(flops=0, bytes_accessed=count * 600000, transcendentals=0),
    )(where, *(pltpu.with_memory_space_constraint(v, pltpu.MemorySpace.HBM) for v in (rhs, diag)))


def local(buf, diags, k):
    sums, here = beside(buf, k)
    images = [
        [(6.0 + diags[p][k, :, tile(t)]) * here[p][t] - sums[p][t] for t in range(TILES)]
        for p in range(4)
    ]
    return images, here


def fill(k, p, q, d, keep, scale, source, one):
    for t in range(TILES):
        s = OMEGA / (6.0 + d[k, :, tile(t)])
        if keep is not None:
            s = s * keep
        g = s * q[t]
        scale[p, k, :, tile(t)] = s
        source[p, k, :, tile(t)] = g
        one[p, k + 1, :, tile(t)] = g


SCRATCH = [
    pltpu.VMEM((4, K, 8, NZ), jnp.float32),
    pltpu.VMEM((4, K, 8, NZ), jnp.float32),
    pltpu.VMEM((4, K + 2, 8, NZ), jnp.float32),
    pltpu.VMEM((4, K + 2, 8, NZ), jnp.float32),
]


def halo(r):
    return (0, 1) if r == 0 else (1, r - 1)


def first_kernel(r, joint, where, pd, ph, p0, p1, p2, *refs):
    if joint:
        together, c, t12, sums, scale, source, one, two = refs
        ch, t2 = together.at[0], together.at[pl.ds(1, 2)]
    else:
        ch, t2, c, t12, sums, scale, source, one, two = refs
    colour, device = where[0], where[1]
    keep = (device > 0).astype(jnp.float32)
    which, at = halo(r)
    qs = ((pd, ph)[which].at[at], p0.at[r], p1.at[r], p2.at[r])
    ds = (pd.at[0], p0.at[NRHS], p1.at[NRHS], p2.at[NRHS])

    def start(k, _):
        for p in range(4):
            q = [qs[p][k, :, tile(t)] for t in range(TILES)]
            fill(k, p, q, ds[p], keep if p == 0 else None, scale, source, one)
        return 0

    lax.fori_loop(0, K, start, 0, unroll=True)
    found = solve(source, scale, one, two)

    def finish(k, carry):
        upper, lower = carry
        images, here = local(found, ds, k)
        mask = owned(k, colour)
        up, low = 0.0, 0.0
        for p in range(4):
            for t in range(TILES):
                value = here[p][t]
                up = up + qs[p][k, :, tile(t)] * value
                low = low + images[p][t] * value
                if p == 0:
                    ch[k, :, tile(t)] = value
                else:
                    c[p - 1, k, :, tile(t)] = value
                if p < 2:
                    t2[p, k, :, tile(t)] = images[p][t]
                else:
                    t12[p - 2, k, :, tile(t)] = images[p][t]
        return upper + jnp.where(mask, up, 0.0), lower + jnp.where(mask, low, 0.0)

    zero = jnp.zeros((8, LANES), jnp.float32)
    upper, lower = lax.fori_loop(0, K, finish, (zero, zero), unroll=True)
    sums[0] = upper
    sums[1] = lower


def estimate(planes, passes):
    return pl.CostEstimate(
        flops=passes * 4 * K * 8 * NZ * 10, bytes_accessed=planes * K * 8 * NZ * 4, transcendentals=0
    )


def first_solve(r, joint, where, *arrays):
    return pl.pallas_call(
        functools.partial(first_kernel, r, joint),
        out_shape=([shape_of(3)] if joint else [shape_of(), shape_of(2)])
        + [shape_of(3), shape_of(2), jax.ShapeDtypeStruct((2, 8, LANES), jnp.float32)],
        in_specs=[SM] + [VM] * 5,
        out_specs=[VM] * (4 if joint else 5),
        scratch_shapes=SCRATCH,
        compiler_params=pltpu.CompilerParams(vmem_limit_bytes=VMEM_LIMIT),
        cost_estimate=estimate(16, SWEEPS + 1),
    )(where, *arrays)


def rows_of(values, count):
    rows = [jnp.sum(v, axis=0, keepdims=True) for v in values]
    rows += [jnp.zeros((1, LANES), jnp.float32)] * (count - len(rows))
    return jnp.concatenate(rows, axis=0)


def plane_of(ref, i):
    return ref.at[i] if len(ref.shape) == 4 else ref


def join_kernel(where, *refs):
    cs, rights, sums, out = refs[:NRHS], refs[NRHS : 2 * NRHS], refs[2 * NRHS : 3 * NRHS], refs[-1]
    colour = where[0]
    zero = jnp.zeros((8, LANES), jnp.float32)
    uppers, lowers = [], []
    for r in range(NRHS):

        def body(k, total, r=r):
            add = 0.0
            for t in range(TILES):
                add = add + cs[r][2, k, :, tile(t)] * plane_of(rights[r], 0)[k, :, tile(t)]
            return total + jnp.where(owned(k, colour), add, 0.0)

        between = lax.fori_loop(0, K, body, zero, unroll=6)
        uppers.append(sums[r][0])
        lowers.append(sums[r][1] - 2.0 * between)
    out[...] = rows_of(uppers + lowers, 8)


def join(where, cs, rights, sums):
    return pl.pallas_call(
        join_kernel,
        out_shape=jax.ShapeDtypeStruct((8, LANES), jnp.float32),
        in_specs=[SM] + [VM] * (3 * NRHS),
        out_specs=VM,
        compiler_params=pltpu.CompilerParams(vmem_limit_bytes=VMEM_LIMIT),
        cost_estimate=estimate(12, 1),
    )(where, *cs, *rights, *sums)


def ratio(table, upper, lower):
    top = jnp.sum(table[upper : upper + 1, :], axis=1, keepdims=True)
    bottom = jnp.sum(table[lower : lower + 1, :], axis=1, keepdims=True)
    return top / bottom


def second_kernel(
    r, where, table, p1, p2, pd, ph, p4, c, cr, tr, t12,
    ca, cm, end, ta, tm, res, sums, scale, source, one, two,
):
    colour, device, count = where[0], where[1], where[2]
    keep = (device < count - 1).astype(jnp.float32)
    cd, td = end.at[0], end.at[1]
    cr = plane_of(cr, 0)
    if tr.shape[0] == 3:
        tr = tr.at[pl.ds(1, 2)]
    alpha = jnp.broadcast_to(ratio(table, r, NRHS + r), (8, LANES))
    which, place_at = halo(r)
    q1, q2, q3, q4 = p1.at[r], p2.at[r], (pd, ph)[which].at[place_at], p4.at[r]
    ds = (p1.at[NRHS], p2.at[NRHS], pd.at[0], p4.at[NRHS])

    def start(k, _):
        for p in range(4):
            values = []
            for t in range(TILES):
                if p == 0:
                    image = t12[0, k, :, tile(t)]
                    q = q1[k, :, tile(t)]
                elif p == 1:
                    image = t12[1, k, :, tile(t)] - cr[k, :, tile(t)]
                    q = q2[k, :, tile(t)]
                elif p == 2:
                    image = tr[0, k, :, tile(t)] - c[2, k, :, tile(t)]
                    q = q3[k, :, tile(t)]
                else:
                    image = tr[1, k, :, tile(t)]
                    q = q4[k, :, tile(t)]
                value = q - alpha * image
                res[p, k, :, tile(t)] = value
                values.append(value)
            fill(k, p, values, ds[p], keep if p == 3 else None, scale, source, one)
        return 0

    lax.fori_loop(0, K, start, 0, unroll=True)
    found = solve(source, scale, one, two)

    def finish(k, carry):
        images, here = local(found, ds, k)
        mask = owned(k, colour)
        adds = [0.0] * 5
        for p in range(4):
            for t in range(TILES):
                value, image, q = here[p][t], images[p][t], res[p, k, :, tile(t)]
                adds[0] = adds[0] + q * value
                adds[1] = adds[1] + image * value
                if p in (1, 2):
                    rest = q - image
                    adds[2] = adds[2] + rest * rest
                    adds[3] = adds[3] + rest * image
                    adds[4] = adds[4] + image * image
                    cm[p - 1, k, :, tile(t)] = value
                    tm[p - 1, k, :, tile(t)] = image
                else:
                    (ca if p == 0 else cd)[k, :, tile(t)] = value
                    (ta if p == 0 else td)[k, :, tile(t)] = image
        return tuple(a + jnp.where(mask, b, 0.0) for a, b in zip(carry, adds))

    zero = jnp.zeros((8, LANES), jnp.float32)
    found_sums = lax.fori_loop(0, K, finish, (zero,) * 5, unroll=True)
    for i in range(5):
        sums[i] = found_sums[i]


def second_solve(r, where, table, *arrays):
    return pl.pallas_call(
        functools.partial(second_kernel, r),
        out_shape=[
            shape_of(),
            shape_of(2),
            shape_of(2),
            shape_of(),
            shape_of(2),
            shape_of(4),
            jax.ShapeDtypeStruct((5, 8, LANES), jnp.float32),
        ],
        in_specs=[SM] + [VM] * 10,
        out_specs=[VM] * 7,
        scratch_shapes=SCRATCH,
        compiler_params=pltpu.CompilerParams(vmem_limit_bytes=VMEM_LIMIT),
        cost_estimate=estimate(28, SWEEPS + 1),
    )(where, table, *arrays)


def join_second_kernel(where, table, *refs):
    out = refs[-1]
    colour, device, count = where[0], where[1], where[2]
    begin = (device == 0).astype(jnp.float32)
    inside = (device < count - 1).astype(jnp.float32)
    zero = jnp.zeros((8, LANES), jnp.float32)
    rows = [[] for _ in range(5)]
    for r in range(NRHS):
        res, ca, end, ta, got, cr, t2, sums = refs[1 + 8 * r : 9 + 8 * r]
        cd, td, cl = end.at[0], end.at[1], got.at[0]
        t0 = t2.at[t2.shape[0] - 1]
        q0 = refs[0].at[r]
        alpha = jnp.broadcast_to(ratio(table, r, NRHS + r), (8, LANES))

        def body(k, carry, res=res, ca=ca, cd=cd, ta=ta, td=td, cl=cl, cr=cr, q0=q0, t0=t0, alpha=alpha):
            between = 0.0
            parts = [[0.0] * 3 for _ in range(3)]
            for t in range(TILES):
                at = (k, slice(None), tile(t))
                between = between + ca[at] * cl[at] + cd[at] * cr[at]
                for n, (q, image) in enumerate(
                    (
                        (res[(0, *at)], ta[at] - cl[at]),
                        (res[(3, *at)], td[at] - cr[at]),
                        (q0[at] - alpha * t0[at], -ca[at]),
                    )
                ):
                    rest = q - image
                    parts[n][0] = parts[n][0] + rest * rest
                    parts[n][1] = parts[n][1] + rest * image
                    parts[n][2] = parts[n][2] + image * image
            adds = [between] + [a + inside * b + begin * c for a, b, c in zip(*parts)]
            mask = owned(k, colour)
            return tuple(a + jnp.where(mask, b, 0.0) for a, b in zip(carry, adds))

        between, *squares = lax.fori_loop(0, K, body, (zero,) * 4, unroll=6)
        rows[0].append(sums[0])
        rows[1].append(sums[1] - between)
        for i in range(3):
            rows[2 + i].append(sums[2 + i] + squares[i])
    out[...] = rows_of([value for row in rows for value in row], 16)


def join_second(where, table, arrays):
    return pl.pallas_call(
        join_second_kernel,
        out_shape=jax.ShapeDtypeStruct((16, LANES), jnp.float32),
        in_specs=[SM] + [VM] * (2 + 8 * NRHS),
        out_specs=VM,
        compiler_params=pltpu.CompilerParams(vmem_limit_bytes=VMEM_LIMIT),
        cost_estimate=estimate(40, 2),
    )(where, table, *arrays)


def last_kernel(where, table, after, *refs):
    norms, full_u, full_q, send_u, send_q, held, sems = refs[-7:]
    colour = where[0]
    low = pl.multiple_of(colour * (WIN - OWN), 8)
    start = pl.multiple_of(colour * OWN, 8)
    rows = []
    pending = []
    for r in range(NRHS):
        t2, c, c3, res, got, ca, cm, ta, tm = refs[1 + 9 * r : 10 + 9 * r]
        c3, c0l, t0l = plane_of(c3, 0), got.at[0], got.at[1]
        t0 = t2.at[t2.shape[0] - 1]
        q0 = refs[0].at[r]
        first = ratio(table, r, NRHS + r)
        second = ratio(after, r, NRHS + r)
        more = second - 1.0
        square, cross, own = (
            jnp.sum(after[i * NRHS + r : i * NRHS + r + 1, :], axis=1, keepdims=True) for i in (2, 3, 4)
        )
        total = square - 2.0 * more * cross + more * more * own
        rows.append(jnp.broadcast_to(jnp.sqrt(jnp.maximum(total, 0.0)), (1, LANES)))
        one = jnp.broadcast_to(first, (8, LANES))
        two = jnp.broadcast_to(second, (8, LANES))
        slot = r % 2
        if r >= 2:
            for copy in pending[r - 2]:
                copy.wait()

        def body(k, _, q0=q0, t0=t0, c=c, c3=c3, res=res, c0l=c0l, ca=ca, cm=cm, t0l=t0l, ta=ta, tm=tm, one=one, two=two, slot=slot):
            for t in range(TILES):
                at = (k, slice(None), tile(t))
                firsts = [c[(0, *at)], c[(1, *at)], c[(2, *at)], c3[at]]
                seconds = [c0l[at], ca[at], cm[(0, *at)], cm[(1, *at)]]
                residuals = [q0[at] - one * t0[at], res[(0, *at)], res[(1, *at)], res[(2, *at)]]
                images = [t0l[at] - ca[at], ta[at] - c0l[at], tm[(0, *at)], tm[(1, *at)]]
                for p in range(4):
                    rows_at = pl.ds(k, 8, stride=K)
                    held[slot, 0, p, t, rows_at, :] = one * firsts[p] + two * seconds[p]
                    held[slot, 1, p, t, rows_at, :] = residuals[p] - two * images[p]
            return 0

        lax.fori_loop(0, K, body, 0, unroll=6)
        copies = []
        half = TILES // 2
        for n, (full, send) in enumerate(((full_u, send_u), (full_q, send_q))):
            for t in range(half):
                copies.append(
                    pltpu.make_async_copy(
                        held.at[slot, n, :, colour * half + t, pl.ds(low, OWN), :],
                        full.at[r, :, pl.ds(start, OWN), tile(t)],
                        sems.at[slot, n, t],
                    )
                )
                copies.append(
                    pltpu.make_async_copy(
                        held.at[slot, n, :, (1 - colour) * half + t, pl.ds(low, OWN), :],
                        send.at[r, :, :, tile(t)],
                        sems.at[slot, n, half + t],
                    )
                )
        for copy in copies:
            copy.start()
        pending.append(copies)
    for copies in pending[max(0, NRHS - 2) :]:
        for copy in copies:
            copy.wait()
    rows += [jnp.zeros((1, LANES), jnp.float32)] * (8 - NRHS)
    norms[...] = jnp.concatenate(rows, axis=0)


def last(where, table, after, arrays):
    full = jax.ShapeDtypeStruct((NRHS, 4, NY, NZ // 2), jnp.float32)
    send = jax.ShapeDtypeStruct((NRHS, 4, OWN, NZ // 2), jnp.float32)
    return pl.pallas_call(
        last_kernel,
        out_shape=[jax.ShapeDtypeStruct((8, LANES), jnp.float32), full, full, send, send],
        in_specs=[SM] + [VM] * (3 + 9 * NRHS),
        out_specs=[VM, HBM, HBM, ANY, ANY],
        scratch_shapes=[
            pltpu.VMEM((2, 2, 4, TILES, WIN, LANES), jnp.float32),
            pltpu.SemaphoreType.DMA((2, 2, TILES)),
        ],
        compiler_params=pltpu.CompilerParams(vmem_limit_bytes=VMEM_LIMIT),
        cost_estimate=estimate(70, 3),
    )(where, table, after, *arrays)


def place_kernel(where, got_u, got_q, in_u, in_q, full_u, full_q, sems):
    start = pl.multiple_of((1 - where[0]) * OWN, 8)
    copies = []
    for n, (got, full) in enumerate(((got_u, full_u), (got_q, full_q))):
        for r in range(NRHS):
            for p in range(4):
                copies.append(
                    pltpu.make_async_copy(
                        got.at[r, p], full.at[r, p, pl.ds(start, OWN)], sems.at[n, r, p]
                    )
                )
    for copy in copies:
        copy.start()
    for copy in copies:
        copy.wait()


def place(where, got_u, got_q, full_u, full_q):
    full = jax.ShapeDtypeStruct((NRHS, 4, NY, NZ // 2), jnp.float32)
    return pl.pallas_call(
        place_kernel,
        out_shape=[full, full],
        in_specs=[SM] + [VM] * 2 + [HBM] * 2,
        out_specs=[HBM] * 2,
        scratch_shapes=[pltpu.SemaphoreType.DMA((2, NRHS, 4))],
        input_output_aliases={3: 0, 4: 1},
        compiler_params=pltpu.CompilerParams(vmem_limit_bytes=4 * 1024 * 1024),
    )(where, got_u, got_q, full_u, full_q)


def everywhere(value):
    for axis in (*reversed(SUB), "colour"):
        count = lax.axis_size(axis)
        others = [
            lax.ppermute(value, axis, [(i, i ^ mask) for i in range(count)])
            for mask in range(1, count)
        ]
        if count == 2:
            value = value + others[0]
        else:
            value = (value + others[0]) + (others[1] + others[2])
    return value


def shards(rhs, diagonal):
    colour = lax.axis_index("colour")
    device = lax.axis_index(SUB)
    total = lax.axis_size(SUB)
    forward = [(i, i + 1) for i in range(total - 1)]
    backward = [(i + 1, i) for i in range(total - 1)]
    where = jnp.stack([colour, device, jnp.int32(total)]).astype(jnp.int32)

    def right(value):
        return lax.ppermute(value, SUB, forward)

    def left(value):
        return lax.ppermute(value, SUB, backward)

    everything = range(NRHS + 1)
    (pd,) = prepare((((3, NRHS), (3, 0)),), where, rhs, diagonal)
    hd = right(pd)
    where, pd = lax.optimization_barrier((where, pd))
    ph, p0 = prepare(
        (tuple((3, r) for r in range(1, NRHS)), tuple((0, r) for r in everything)),
        where, rhs, diagonal,
    )
    hh = right(ph)
    p4 = left(p0)
    p1, p2 = prepare(tuple(tuple((plane, r) for r in everything) for plane in (1, 2)), where, rhs, diagonal)

    together, c0, inner0, sums0 = first_solve(0, True, where, hd, pd, p0, p1, p2)
    ahead = left(together)
    ch1, t1, c1, inner1, sums1 = first_solve(1, False, where, hd, hh, p0, p1, p2)
    ch1 = left(ch1)
    hh, p4 = lax.optimization_barrier((hh, p4))
    ch2, t2, c2, inner2, sums2 = first_solve(2, False, where, hd, hh, p0, p1, p2)
    ch2 = left(ch2)
    t = (together, t1, t2)
    c, cr = (c0, c1, c2), (ahead, ch1, ch2)
    inner = (inner0, inner1, inner2)
    table = everywhere(join(where, c, cr, (sums0, sums1, sums2)))
    table, t1, t2 = lax.optimization_barrier((table, t1, t2))
    tr = (ahead, left(t1), left(t2))
    seconds = []
    sent = []
    for r in range(NRHS):
        out = second_solve(r, where, table, p1, p2, pd, ph, p4, c[r], cr[r], tr[r], inner[r])
        seconds.append(out)
        sent.append((right(out[2]), left(out[0])))
    ca, cm, end, ta, tm, res, sums = zip(*seconds)
    got, cr1 = zip(*sent)
    arrays = [
        a
        for r in range(NRHS)
        for a in (res[r], ca[r], end[r], ta[r], got[r], cr1[r], t[r], sums[r])
    ]
    after = everywhere(join_second(where, table, [p0, *arrays]))
    arrays = [
        a
        for r in range(NRHS)
        for a in (t[r], c[r], cr[r], res[r], got[r], ca[r], cm[r], ta[r], tm[r])
    ]
    norms, full_u, full_q, send_u, send_q = last(where, table, after, [p0, *arrays])
    pairs = [(0, 1), (1, 0)]
    got_u, got_q = (lax.ppermute(v, "colour", pairs) for v in (send_u, send_q))
    full_u, full_q = place(where, got_u, got_q, full_u, full_q)
    return full_u, full_q, norms[:NRHS, 0]


def solution(mesh):
    torus = Mesh(
        mesh.devices.reshape(mesh.shape["colour"], 4, 4, 4), ("colour", "sub_0", "sub_1", "sub_2")
    )
    return jax.shard_map(
        shards,
        mesh=torus,
        in_specs=(P(None, SUB, None, None), P(SUB, None, None)),
        out_specs=(P(None, SUB, None, "colour"), P(None, SUB, None, "colour"), P()),
        check_vma=False,
    )
```

```python
import functools

import jax
import jax.numpy as jnp
from jax import lax
from jax.experimental import pallas as pl
from jax.experimental.pallas import tpu as pltpu
from jax.sharding import Mesh
from jax.sharding import PartitionSpec as P

OMEGA = 0.8
SWEEPS = 8
NY = 256
NZ = 512
NRHS = 3
OWN = 128
WIN = 144
K = WIN // 8
LANES = 128
TILES = NZ // LANES
SUB = ("sub_0", "sub_1", "sub_2")
VMEM_LIMIT = 12 * 1024 * 1024


def powers():
    total = [0.0] * SWEEPS
    power = [1.0]
    for _ in range(SWEEPS):
        for i, value in enumerate(power):
            total[i] += value
        longer = [0.0] * (len(power) + 1)
        for i, value in enumerate(power):
            longer[i] += (1.0 - OMEGA) * value
            longer[i + 1] += value
        power = longer
    return total


COEFFICIENTS = powers()
PLANE = (K, 8, NZ)
VM = pl.BlockSpec(memory_space=pltpu.VMEM)
SM = pl.BlockSpec(memory_space=pltpu.SMEM)
ANY = pl.BlockSpec(memory_space=pl.ANY)
HBM = pl.BlockSpec(memory_space=pltpu.MemorySpace.HBM)


def shape_of(*lead):
    return jax.ShapeDtypeStruct((*lead, *PLANE), jnp.float32)


def tile(t):
    return slice(t * LANES, (t + 1) * LANES)


def lanes():
    return lax.broadcasted_iota(jnp.int32, (8, LANES), 1)


def sublanes():
    return lax.broadcasted_iota(jnp.int32, (8, LANES), 0)


def owned(k, colour):
    row = sublanes() * K + k - colour * (WIN - OWN)
    return (row >= 0) & (row < OWN)


def close_edges(buf):
    sub = sublanes()
    for p in range(4):
        for t in range(TILES):
            last = pltpu.roll(buf[p, K, :, tile(t)], 1, 0)
            buf[p, 0, :, tile(t)] = jnp.where(sub == 0, 0.0, last)
            first = pltpu.roll(buf[p, 1, :, tile(t)], 7, 0)
            buf[p, K + 1, :, tile(t)] = jnp.where(sub == 7, 0.0, first)


def beside(buf, k):
    lane = lanes()
    first, last = lane == 0, lane == LANES - 1
    here = [[buf[p, k + 1, :, tile(t)] for t in range(TILES)] for p in range(4)]
    sums = []
    for p in range(4):
        up = [pltpu.roll(v, 1, 1) for v in here[p]]
        down = [pltpu.roll(v, LANES - 1, 1) for v in here[p]]
        row = []
        for t in range(TILES):
            total = jnp.where(first, up[t - 1] if t else 0.0, up[t])
            total = total + jnp.where(last, down[t + 1] if t + 1 < TILES else 0.0, down[t])
            total = total + (buf[p, k, :, tile(t)] + buf[p, k + 2, :, tile(t)])
            if p == 0:
                total = total + here[1][t]
            elif p == 3:
                total = total + here[2][t]
            else:
                total = total + (here[p - 1][t] + here[p + 1][t])
            row.append(total)
        sums.append(row)
    return sums, here


def solve(source, scale, one, two):
    close_edges(one)
    bufs = (one, two)
    for step, power in enumerate(range(SWEEPS - 2, -1, -1)):
        src, dst = bufs[step % 2], bufs[1 - step % 2]
        factor = COEFFICIENTS[power]

        def body(k, _, src=src, dst=dst, factor=factor):
            sums, _ = beside(src, k)
            for p in range(4):
                for t in range(TILES):
                    dst[p, k + 1, :, tile(t)] = (
                        scale[p, k, :, tile(t)] * sums[p][t]
                        + factor * source[p, k, :, tile(t)]
                    )
            return 0

        lax.fori_loop(0, K, body, 0, unroll=True)
        close_edges(dst)
    return bufs[(SWEEPS - 1) % 2]


def prepare_kernel(packs, where, rhs, diag, *refs):
    outs, (held, sem) = refs[: len(packs)], refs[len(packs) :]
    low = pl.multiple_of(where[0] * (NY - WIN), 8)
    places = [(out, i, *item) for out, pack in zip(outs, packs) for i, item in enumerate(pack)]
    copies = []
    for n, (_, _, plane, r) in enumerate(places):
        for t in range(TILES):
            if r < NRHS:
                src = rhs.at[r, plane, pl.ds(low, WIN), tile(t)]
            else:
                src = diag.at[plane, pl.ds(low, WIN), tile(t)]
            copies.append(pltpu.make_async_copy(src, held.at[n, t], sem.at[n, t]))
    for copy in copies:
        copy.start()
    for n, (out, i, _, _) in enumerate(places):
        for t in range(TILES):
            copies[n * TILES + t].wait()
            for k in range(K):
                out[i, k, :, tile(t)] = held[n, t, pl.ds(k, 8, stride=K), :]


def prepare(packs, where, rhs, diag):
    count = sum(len(pack) for pack in packs)
    return pl.pallas_call(
        functools.partial(prepare_kernel, packs),
        out_shape=[shape_of(len(pack)) for pack in packs],
        in_specs=[SM, HBM, HBM],
        out_specs=[VM] * len(packs),
        scratch_shapes=[
            pltpu.VMEM((count, TILES, WIN, LANES), jnp.float32),
            pltpu.SemaphoreType.DMA((count, TILES)),
        ],
        compiler_params=pltpu.CompilerParams(vmem_limit_bytes=VMEM_LIMIT),
        cost_estimate=pl.CostEstimate(flops=0, bytes_accessed=0, transcendentals=0),
    )(where, *(pltpu.with_memory_space_constraint(v, pltpu.MemorySpace.HBM) for v in (rhs, diag)))


def local(buf, diags, k):
    sums, here = beside(buf, k)
    images = [
        [(6.0 + diags[p][k, :, tile(t)]) * here[p][t] - sums[p][t] for t in range(TILES)]
        for p in range(4)
    ]
    return images, here


def fill(k, p, q, d, keep, scale, source, one):
    for t in range(TILES):
        s = OMEGA / (6.0 + d[k, :, tile(t)])
        if keep is not None:
            s = s * keep
        g = s * q[t]
        scale[p, k, :, tile(t)] = s
        source[p, k, :, tile(t)] = g
        one[p, k + 1, :, tile(t)] = g


SCRATCH = [
    pltpu.VMEM((4, K, 8, NZ), jnp.float32),
    pltpu.VMEM((4, K, 8, NZ), jnp.float32),
    pltpu.VMEM((4, K + 2, 8, NZ), jnp.float32),
    pltpu.VMEM((4, K + 2, 8, NZ), jnp.float32),
]


def halo(r):
    return (0, 1) if r == 0 else (1, r - 1)


def first_kernel(r, joint, where, pd, ph, p0, p1, p2, *refs):
    if joint:
        together, c, t12, sums, scale, source, one, two = refs
        ch, t2 = together.at[0], together.at[pl.ds(1, 2)]
    else:
        ch, t2, c, t12, sums, scale, source, one, two = refs
    colour, device = where[0], where[1]
    keep = (device > 0).astype(jnp.float32)
    which, at = halo(r)
    qs = ((pd, ph)[which].at[at], p0.at[r], p1.at[r], p2.at[r])
    ds = (pd.at[0], p0.at[NRHS], p1.at[NRHS], p2.at[NRHS])

    def start(k, _):
        for p in range(4):
            q = [qs[p][k, :, tile(t)] for t in range(TILES)]
            fill(k, p, q, ds[p], keep if p == 0 else None, scale, source, one)
        return 0

    lax.fori_loop(0, K, start, 0, unroll=True)
    found = solve(source, scale, one, two)

    def finish(k, carry):
        upper, lower = carry
        images, here = local(found, ds, k)
        mask = owned(k, colour)
        up, low = 0.0, 0.0
        for p in range(4):
            for t in range(TILES):
                value = here[p][t]
                up = up + qs[p][k, :, tile(t)] * value
                low = low + images[p][t] * value
                if p == 0:
                    ch[k, :, tile(t)] = value
                else:
                    c[p - 1, k, :, tile(t)] = value
                if p < 2:
                    t2[p, k, :, tile(t)] = images[p][t]
                else:
                    t12[p - 2, k, :, tile(t)] = images[p][t]
        return upper + jnp.where(mask, up, 0.0), lower + jnp.where(mask, low, 0.0)

    zero = jnp.zeros((8, LANES), jnp.float32)
    upper, lower = lax.fori_loop(0, K, finish, (zero, zero), unroll=True)
    sums[0] = upper
    sums[1] = lower


def estimate(planes, passes):
    return pl.CostEstimate(
        flops=passes * 4 * K * 8 * NZ * 10, bytes_accessed=planes * K * 8 * NZ * 4, transcendentals=0
    )


def first_solve(r, joint, where, *arrays):
    return pl.pallas_call(
        functools.partial(first_kernel, r, joint),
        out_shape=([shape_of(3)] if joint else [shape_of(), shape_of(2)])
        + [shape_of(3), shape_of(2), jax.ShapeDtypeStruct((2, 8, LANES), jnp.float32)],
        in_specs=[SM] + [VM] * 5,
        out_specs=[VM] * (4 if joint else 5),
        scratch_shapes=SCRATCH,
        compiler_params=pltpu.CompilerParams(vmem_limit_bytes=VMEM_LIMIT),
        cost_estimate=estimate(16, SWEEPS + 1),
    )(where, *arrays)


def packed(values, out):
    rows = [jnp.sum(v, axis=0, keepdims=True) for v in values]
    rows += [jnp.zeros((1, LANES), jnp.float32)] * (16 - len(rows))
    totals = jnp.sum(jnp.concatenate(rows, axis=0), axis=1, keepdims=True)
    own = lax.broadcasted_iota(jnp.int32, (16, LANES), 0) == lax.broadcasted_iota(jnp.int32, (16, LANES), 1)
    line = jnp.sum(jnp.where(own, totals, 0.0), axis=0, keepdims=True)
    out[...] = jnp.broadcast_to(line, out.shape)


def plane_of(ref, i):
    return ref.at[i] if len(ref.shape) == 4 else ref


def join_kernel(where, *refs):
    cs, rights, sums, out = refs[:NRHS], refs[NRHS : 2 * NRHS], refs[2 * NRHS : 3 * NRHS], refs[-1]
    colour = where[0]
    zero = jnp.zeros((8, LANES), jnp.float32)
    uppers, lowers = [], []
    for r in range(NRHS):

        def body(k, total, r=r):
            add = 0.0
            for t in range(TILES):
                add = add + cs[r][2, k, :, tile(t)] * plane_of(rights[r], 0)[k, :, tile(t)]
            return total + jnp.where(owned(k, colour), add, 0.0)

        between = lax.fori_loop(0, K, body, zero, unroll=6)
        uppers.append(sums[r][0])
        lowers.append(sums[r][1] - 2.0 * between)
    packed(uppers + lowers, out)


def join(count, where, cs, rights, sums):
    return pl.pallas_call(
        join_kernel,
        out_shape=jax.ShapeDtypeStruct((count, LANES), jnp.float32),
        in_specs=[SM] + [VM] * (3 * NRHS),
        out_specs=VM,
        compiler_params=pltpu.CompilerParams(vmem_limit_bytes=VMEM_LIMIT),
        cost_estimate=estimate(12, 1),
    )(where, *cs, *rights, *sums)


def pick(table, index):
    line = jnp.sum(table[...], axis=0, keepdims=True)
    lane = lax.broadcasted_iota(jnp.int32, (1, LANES), 1)
    return jnp.sum(jnp.where(lane == index, line, 0.0), axis=1, keepdims=True)


def ratio(table, upper, lower):
    return pick(table, upper) / pick(table, lower)


def second_kernel(
    r, where, table, p1, p2, pd, ph, p4, c, cr, tr, t12,
    ca, cm, end, ta, tm, res, sums, scale, source, one, two,
):
    colour, device, count = where[0], where[1], where[2]
    keep = (device < count - 1).astype(jnp.float32)
    cd, td = end.at[0], end.at[1]
    cr = plane_of(cr, 0)
    if tr.shape[0] == 3:
        tr = tr.at[pl.ds(1, 2)]
    alpha = jnp.broadcast_to(ratio(table, r, NRHS + r), (8, LANES))
    which, place_at = halo(r)
    q1, q2, q3, q4 = p1.at[r], p2.at[r], (pd, ph)[which].at[place_at], p4.at[r]
    ds = (p1.at[NRHS], p2.at[NRHS], pd.at[0], p4.at[NRHS])

    def start(k, _):
        for p in range(4):
            values = []
            for t in range(TILES):
                if p == 0:
                    image = t12[0, k, :, tile(t)]
                    q = q1[k, :, tile(t)]
                elif p == 1:
                    image = t12[1, k, :, tile(t)] - cr[k, :, tile(t)]
                    q = q2[k, :, tile(t)]
                elif p == 2:
                    image = tr[0, k, :, tile(t)] - c[2, k, :, tile(t)]
                    q = q3[k, :, tile(t)]
                else:
                    image = tr[1, k, :, tile(t)]
                    q = q4[k, :, tile(t)]
                value = q - alpha * image
                res[p, k, :, tile(t)] = value
                values.append(value)
            fill(k, p, values, ds[p], keep if p == 3 else None, scale, source, one)
        return 0

    lax.fori_loop(0, K, start, 0, unroll=True)
    found = solve(source, scale, one, two)

    def finish(k, carry):
        images, here = local(found, ds, k)
        mask = owned(k, colour)
        adds = [0.0] * 5
        for p in range(4):
            for t in range(TILES):
                value, image, q = here[p][t], images[p][t], res[p, k, :, tile(t)]
                adds[0] = adds[0] + q * value
                adds[1] = adds[1] + image * value
                if p in (1, 2):
                    rest = q - image
                    adds[2] = adds[2] + rest * rest
                    adds[3] = adds[3] + rest * image
                    adds[4] = adds[4] + image * image
                    cm[p - 1, k, :, tile(t)] = value
                    tm[p - 1, k, :, tile(t)] = image
                else:
                    (ca if p == 0 else cd)[k, :, tile(t)] = value
                    (ta if p == 0 else td)[k, :, tile(t)] = image
        return tuple(a + jnp.where(mask, b, 0.0) for a, b in zip(carry, adds))

    zero = jnp.zeros((8, LANES), jnp.float32)
    found_sums = lax.fori_loop(0, K, finish, (zero,) * 5, unroll=True)
    for i in range(5):
        sums[i] = found_sums[i]


def second_solve(r, where, table, *arrays):
    return pl.pallas_call(
        functools.partial(second_kernel, r),
        out_shape=[
            shape_of(),
            shape_of(2),
            shape_of(2),
            shape_of(),
            shape_of(2),
            shape_of(4),
            jax.ShapeDtypeStruct((5, 8, LANES), jnp.float32),
        ],
        in_specs=[SM] + [VM] * 10,
        out_specs=[VM] * 7,
        scratch_shapes=SCRATCH,
        compiler_params=pltpu.CompilerParams(vmem_limit_bytes=VMEM_LIMIT),
        cost_estimate=estimate(28, SWEEPS + 1),
    )(where, table, *arrays)


def join_second_kernel(where, table, *refs):
    out = refs[-1]
    colour, device, count = where[0], where[1], where[2]
    begin = (device == 0).astype(jnp.float32)
    inside = (device < count - 1).astype(jnp.float32)
    zero = jnp.zeros((8, LANES), jnp.float32)
    rows = [[] for _ in range(5)]
    for r in range(NRHS):
        res, ca, end, ta, got, cr, t2, sums = refs[1 + 8 * r : 9 + 8 * r]
        cd, td, cl = end.at[0], end.at[1], got.at[0]
        t0 = t2.at[t2.shape[0] - 1]
        q0 = refs[0].at[r]
        alpha = jnp.broadcast_to(ratio(table, r, NRHS + r), (8, LANES))

        def body(k, carry, res=res, ca=ca, cd=cd, ta=ta, td=td, cl=cl, cr=cr, q0=q0, t0=t0, alpha=alpha):
            between = 0.0
            parts = [[0.0] * 3 for _ in range(3)]
            for t in range(TILES):
                at = (k, slice(None), tile(t))
                between = between + ca[at] * cl[at] + cd[at] * cr[at]
                for n, (q, image) in enumerate(
                    (
                        (res[(0, *at)], ta[at] - cl[at]),
                        (res[(3, *at)], td[at] - cr[at]),
                        (q0[at] - alpha * t0[at], -ca[at]),
                    )
                ):
                    rest = q - image
                    parts[n][0] = parts[n][0] + rest * rest
                    parts[n][1] = parts[n][1] + rest * image
                    parts[n][2] = parts[n][2] + image * image
            adds = [between] + [a + inside * b + begin * c for a, b, c in zip(*parts)]
            mask = owned(k, colour)
            return tuple(a + jnp.where(mask, b, 0.0) for a, b in zip(carry, adds))

        between, *squares = lax.fori_loop(0, K, body, (zero,) * 4, unroll=6)
        rows[0].append(sums[0])
        rows[1].append(sums[1] - between)
        for i in range(3):
            rows[2 + i].append(sums[2 + i] + squares[i])
    packed([value for row in rows for value in row], out)


def join_second(count, where, table, arrays):
    return pl.pallas_call(
        join_second_kernel,
        out_shape=jax.ShapeDtypeStruct((count, LANES), jnp.float32),
        in_specs=[SM] + [VM] * (2 + 8 * NRHS),
        out_specs=VM,
        compiler_params=pltpu.CompilerParams(vmem_limit_bytes=VMEM_LIMIT),
        cost_estimate=estimate(40, 2),
    )(where, table, *arrays)


def last_kernel(where, table, after, *refs):
    norms, full_u, full_q, send_u, send_q, held, sems = refs[-7:]
    colour = where[0]
    low = pl.multiple_of(colour * (WIN - OWN), 8)
    start = pl.multiple_of(colour * OWN, 8)
    rows = []
    pending = []
    for r in range(NRHS):
        t2, c, c3, res, got, ca, cm, ta, tm = refs[1 + 9 * r : 10 + 9 * r]
        c3, c0l, t0l = plane_of(c3, 0), got.at[0], got.at[1]
        t0 = t2.at[t2.shape[0] - 1]
        q0 = refs[0].at[r]
        first = ratio(table, r, NRHS + r)
        second = ratio(after, r, NRHS + r)
        more = second - 1.0
        square, cross, own = (
            pick(after, i * NRHS + r) for i in (2, 3, 4)
        )
        total = square - 2.0 * more * cross + more * more * own
        rows.append(jnp.broadcast_to(jnp.sqrt(jnp.maximum(total, 0.0)), (1, LANES)))
        one = jnp.broadcast_to(first, (8, LANES))
        two = jnp.broadcast_to(second, (8, LANES))
        slot = r % 2
        if r >= 2:
            for copy in pending[r - 2]:
                copy.wait()

        def body(k, _, q0=q0, t0=t0, c=c, c3=c3, res=res, c0l=c0l, ca=ca, cm=cm, t0l=t0l, ta=ta, tm=tm, one=one, two=two, slot=slot):
            for t in range(TILES):
                at = (k, slice(None), tile(t))
                firsts = [c[(0, *at)], c[(1, *at)], c[(2, *at)], c3[at]]
                seconds = [c0l[at], ca[at], cm[(0, *at)], cm[(1, *at)]]
                residuals = [q0[at] - one * t0[at], res[(0, *at)], res[(1, *at)], res[(2, *at)]]
                images = [t0l[at] - ca[at], ta[at] - c0l[at], tm[(0, *at)], tm[(1, *at)]]
                for p in range(4):
                    rows_at = pl.ds(k, 8, stride=K)
                    held[slot, 0, p, t, rows_at, :] = one * firsts[p] + two * seconds[p]
                    held[slot, 1, p, t, rows_at, :] = residuals[p] - two * images[p]
            return 0

        lax.fori_loop(0, K, body, 0, unroll=6)
        copies = []
        half = TILES // 2
        for n, (full, send) in enumerate(((full_u, send_u), (full_q, send_q))):
            for t in range(half):
                copies.append(
                    pltpu.make_async_copy(
                        held.at[slot, n, :, colour * half + t, pl.ds(low, OWN), :],
                        full.at[r, :, pl.ds(start, OWN), tile(t)],
                        sems.at[slot, n, t],
                    )
                )
                copies.append(
                    pltpu.make_async_copy(
                        held.at[slot, n, :, (1 - colour) * half + t, pl.ds(low, OWN), :],
                        send.at[r, :, :, tile(t)],
                        sems.at[slot, n, half + t],
                    )
                )
        for copy in copies:
            copy.start()
        pending.append(copies)
    for copies in pending[max(0, NRHS - 2) :]:
        for copy in copies:
            copy.wait()
    rows += [jnp.zeros((1, LANES), jnp.float32)] * (8 - NRHS)
    norms[...] = jnp.concatenate(rows, axis=0)


def last(where, table, after, arrays):
    full = jax.ShapeDtypeStruct((NRHS, 4, NY, NZ // 2), jnp.float32)
    send = jax.ShapeDtypeStruct((NRHS, 4, OWN, NZ // 2), jnp.float32)
    return pl.pallas_call(
        last_kernel,
        out_shape=[jax.ShapeDtypeStruct((8, LANES), jnp.float32), full, full, send, send],
        in_specs=[SM] + [VM] * (3 + 9 * NRHS),
        out_specs=[VM, HBM, HBM, ANY, ANY],
        scratch_shapes=[
            pltpu.VMEM((2, 2, 4, TILES, WIN, LANES), jnp.float32),
            pltpu.SemaphoreType.DMA((2, 2, TILES)),
        ],
        compiler_params=pltpu.CompilerParams(vmem_limit_bytes=VMEM_LIMIT),
        cost_estimate=estimate(70, 3),
    )(where, table, after, *arrays)


def place_kernel(where, got_u, got_q, in_u, in_q, full_u, full_q, sems):
    start = pl.multiple_of((1 - where[0]) * OWN, 8)
    copies = []
    for n, (got, full) in enumerate(((got_u, full_u), (got_q, full_q))):
        for r in range(NRHS):
            for p in range(4):
                copies.append(
                    pltpu.make_async_copy(
                        got.at[r, p], full.at[r, p, pl.ds(start, OWN)], sems.at[n, r, p]
                    )
                )
    for copy in copies:
        copy.start()
    for copy in copies:
        copy.wait()


def place(where, got_u, got_q, full_u, full_q):
    full = jax.ShapeDtypeStruct((NRHS, 4, NY, NZ // 2), jnp.float32)
    return pl.pallas_call(
        place_kernel,
        out_shape=[full, full],
        in_specs=[SM] + [VM] * 2 + [HBM] * 2,
        out_specs=[HBM] * 2,
        scratch_shapes=[pltpu.SemaphoreType.DMA((2, NRHS, 4))],
        input_output_aliases={3: 0, 4: 1},
        compiler_params=pltpu.CompilerParams(vmem_limit_bytes=4 * 1024 * 1024),
    )(where, got_u, got_q, full_u, full_q)


def everywhere(lines):
    return lax.all_to_all(lines, ("colour", *SUB), split_axis=0, concat_axis=0, tiled=True)


def shards(rhs, diagonal):
    colour = lax.axis_index("colour")
    device = lax.axis_index(SUB)
    total = lax.axis_size(SUB)
    devices = total * lax.axis_size("colour")
    forward = [(i, i + 1) for i in range(total - 1)]
    backward = [(i + 1, i) for i in range(total - 1)]
    where = jnp.stack([colour, device, jnp.int32(total)]).astype(jnp.int32)

    def right(value):
        return lax.ppermute(value, SUB, forward)

    def left(value):
        return lax.ppermute(value, SUB, backward)

    everything = range(NRHS + 1)
    (pd,) = prepare((((3, NRHS), (3, 0)),), where, rhs, diagonal)
    hd = right(pd)
    where, pd = lax.optimization_barrier((where, pd))
    ph, p0 = prepare(
        (tuple((3, r) for r in range(1, NRHS)), tuple((0, r) for r in everything)),
        where, rhs, diagonal,
    )
    hh = right(ph)
    p4 = left(p0)
    p1, p2 = prepare(tuple(tuple((plane, r) for r in everything) for plane in (1, 2)), where, rhs, diagonal)

    together, c0, inner0, sums0 = first_solve(0, True, where, hd, pd, p0, p1, p2)
    ahead = left(together)
    ch1, t1, c1, inner1, sums1 = first_solve(1, False, where, hd, hh, p0, p1, p2)
    ch1 = left(ch1)
    hh, p4 = lax.optimization_barrier((hh, p4))
    ch2, t2, c2, inner2, sums2 = first_solve(2, False, where, hd, hh, p0, p1, p2)
    ch2 = left(ch2)
    t = (together, t1, t2)
    c, cr = (c0, c1, c2), (ahead, ch1, ch2)
    inner = (inner0, inner1, inner2)
    table = everywhere(join(devices, where, c, cr, (sums0, sums1, sums2)))
    table, t1, t2 = lax.optimization_barrier((table, t1, t2))
    tr = (ahead, left(t1), left(t2))
    seconds = []
    sent = []
    for r in range(NRHS):
        out = second_solve(r, where, table, p1, p2, pd, ph, p4, c[r], cr[r], tr[r], inner[r])
        seconds.append(out)
        sent.append((right(out[2]), left(out[0])))
    ca, cm, end, ta, tm, res, sums = zip(*seconds)
    got, cr1 = zip(*sent)
    arrays = [
        a
        for r in range(NRHS)
        for a in (res[r], ca[r], end[r], ta[r], got[r], cr1[r], t[r], sums[r])
    ]
    after = everywhere(join_second(devices, where, table, [p0, *arrays]))
    arrays = [
        a
        for r in range(NRHS)
        for a in (t[r], c[r], cr[r], res[r], got[r], ca[r], cm[r], ta[r], tm[r])
    ]
    norms, full_u, full_q, send_u, send_q = last(where, table, after, [p0, *arrays])
    pairs = [(0, 1), (1, 0)]
    got_u, got_q = (lax.ppermute(v, "colour", pairs) for v in (send_u, send_q))
    full_u, full_q = place(where, got_u, got_q, full_u, full_q)
    return full_u, full_q, norms[:NRHS, 0]


def solution(mesh):
    torus = Mesh(
        mesh.devices.reshape(mesh.shape["colour"], 4, 4, 4), ("colour", "sub_0", "sub_1", "sub_2")
    )
    return jax.shard_map(
        shards,
        mesh=torus,
        in_specs=(P(None, SUB, None, None), P(SUB, None, None)),
        out_specs=(P(None, SUB, None, "colour"), P(None, SUB, None, "colour"), P()),
        check_vma=False,
    )
```

```python
import functools

import jax
import jax.numpy as jnp
from jax import lax
from jax.experimental import pallas as pl
from jax.experimental.pallas import tpu as pltpu
from jax.sharding import Mesh
from jax.sharding import PartitionSpec as P

OMEGA = 0.8
SWEEPS = 8
NY = 256
NZ = 512
NRHS = 3
OWN = 128
WIN = 144
K = WIN // 8
LANES = 128
TILES = NZ // LANES
SUB = ("sub_0", "sub_1", "sub_2")
VMEM_LIMIT = 12 * 1024 * 1024


def powers():
    total = [0.0] * SWEEPS
    power = [1.0]
    for _ in range(SWEEPS):
        for i, value in enumerate(power):
            total[i] += value
        longer = [0.0] * (len(power) + 1)
        for i, value in enumerate(power):
            longer[i] += (1.0 - OMEGA) * value
            longer[i + 1] += value
        power = longer
    return total


COEFFICIENTS = powers()
PLANE = (K, 8, NZ)
VM = pl.BlockSpec(memory_space=pltpu.VMEM)
SM = pl.BlockSpec(memory_space=pltpu.SMEM)
ANY = pl.BlockSpec(memory_space=pl.ANY)
HBM = pl.BlockSpec(memory_space=pltpu.MemorySpace.HBM)


def shape_of(*lead):
    return jax.ShapeDtypeStruct((*lead, *PLANE), jnp.float32)


def tile(t):
    return slice(t * LANES, (t + 1) * LANES)


def lanes():
    return lax.broadcasted_iota(jnp.int32, (8, LANES), 1)


def sublanes():
    return lax.broadcasted_iota(jnp.int32, (8, LANES), 0)


def owned(k, colour):
    row = sublanes() * K + k - colour * (WIN - OWN)
    return (row >= 0) & (row < OWN)


def close_edges(buf):
    sub = sublanes()
    for p in range(4):
        for t in range(TILES):
            last = pltpu.roll(buf[p, K, :, tile(t)], 1, 0)
            buf[p, 0, :, tile(t)] = jnp.where(sub == 0, 0.0, last)
            first = pltpu.roll(buf[p, 1, :, tile(t)], 7, 0)
            buf[p, K + 1, :, tile(t)] = jnp.where(sub == 7, 0.0, first)


def beside(buf, k):
    lane = lanes()
    first, last = lane == 0, lane == LANES - 1
    here = [[buf[p, k + 1, :, tile(t)] for t in range(TILES)] for p in range(4)]
    sums = []
    for p in range(4):
        up = [pltpu.roll(v, 1, 1) for v in here[p]]
        down = [pltpu.roll(v, LANES - 1, 1) for v in here[p]]
        row = []
        for t in range(TILES):
            total = jnp.where(first, up[t - 1] if t else 0.0, up[t])
            total = total + jnp.where(last, down[t + 1] if t + 1 < TILES else 0.0, down[t])
            total = total + (buf[p, k, :, tile(t)] + buf[p, k + 2, :, tile(t)])
            if p == 0:
                total = total + here[1][t]
            elif p == 3:
                total = total + here[2][t]
            else:
                total = total + (here[p - 1][t] + here[p + 1][t])
            row.append(total)
        sums.append(row)
    return sums, here


def solve(source, scale, one, two):
    close_edges(one)
    bufs = (one, two)
    for step, power in enumerate(range(SWEEPS - 2, -1, -1)):
        src, dst = bufs[step % 2], bufs[1 - step % 2]
        factor = COEFFICIENTS[power]

        def body(k, _, src=src, dst=dst, factor=factor):
            sums, _ = beside(src, k)
            for p in range(4):
                for t in range(TILES):
                    dst[p, k + 1, :, tile(t)] = (
                        scale[p, k, :, tile(t)] * sums[p][t]
                        + factor * source[p, k, :, tile(t)]
                    )
            return 0

        lax.fori_loop(0, K, body, 0, unroll=True)
        close_edges(dst)
    return bufs[(SWEEPS - 1) % 2]


def prepare_kernel(packs, where, rhs, diag, *refs):
    outs, (held, sem) = refs[: len(packs)], refs[len(packs) :]
    low = pl.multiple_of(where[0] * (NY - WIN), 8)
    places = [(out, i, *item) for out, pack in zip(outs, packs) for i, item in enumerate(pack)]
    copies = []
    for n, (_, _, plane, r) in enumerate(places):
        for t in range(TILES):
            if r < NRHS:
                src = rhs.at[r, plane, pl.ds(low, WIN), tile(t)]
            else:
                src = diag.at[plane, pl.ds(low, WIN), tile(t)]
            copies.append(pltpu.make_async_copy(src, held.at[n, t], sem.at[n, t]))
    for copy in copies:
        copy.start()
    for n, (out, i, _, _) in enumerate(places):
        for t in range(TILES):
            copies[n * TILES + t].wait()
            for k in range(K):
                out[i, k, :, tile(t)] = held[n, t, pl.ds(k, 8, stride=K), :]


def prepare(packs, where, rhs, diag):
    count = sum(len(pack) for pack in packs)
    return pl.pallas_call(
        functools.partial(prepare_kernel, packs),
        out_shape=[shape_of(len(pack)) for pack in packs],
        in_specs=[SM, HBM, HBM],
        out_specs=[VM] * len(packs),
        scratch_shapes=[
            pltpu.VMEM((count, TILES, WIN, LANES), jnp.float32),
            pltpu.SemaphoreType.DMA((count, TILES)),
        ],
        compiler_params=pltpu.CompilerParams(vmem_limit_bytes=VMEM_LIMIT),
        cost_estimate=pl.CostEstimate(flops=0, bytes_accessed=0, transcendentals=0),
    )(where, *(pltpu.with_memory_space_constraint(v, pltpu.MemorySpace.HBM) for v in (rhs, diag)))


def local(buf, diags, k):
    sums, here = beside(buf, k)
    images = [
        [(6.0 + diags[p][k, :, tile(t)]) * here[p][t] - sums[p][t] for t in range(TILES)]
        for p in range(4)
    ]
    return images, here


def fill(k, p, q, d, keep, scale, source, one):
    for t in range(TILES):
        s = OMEGA / (6.0 + d[k, :, tile(t)])
        if keep is not None:
            s = s * keep
        g = s * q[t]
        scale[p, k, :, tile(t)] = s
        source[p, k, :, tile(t)] = g
        one[p, k + 1, :, tile(t)] = g


SCRATCH = [
    pltpu.VMEM((4, K, 8, NZ), jnp.float32),
    pltpu.VMEM((4, K, 8, NZ), jnp.float32),
    pltpu.VMEM((4, K + 2, 8, NZ), jnp.float32),
    pltpu.VMEM((4, K + 2, 8, NZ), jnp.float32),
]


def halo(r):
    return (0, 1) if r == 0 else (1, r - 1)


def first_kernel(r, joint, where, pd, ph, p0, p1, p2, *refs):
    if joint:
        together, c, t12, sums, scale, source, one, two = refs
        ch, t2 = together.at[0], together.at[pl.ds(1, 2)]
    else:
        ch, t2, c, t12, sums, scale, source, one, two = refs
    colour, device = where[0], where[1]
    keep = (device > 0).astype(jnp.float32)
    which, at = halo(r)
    qs = ((pd, ph)[which].at[at], p0.at[r], p1.at[r], p2.at[r])
    ds = (pd.at[0], p0.at[NRHS], p1.at[NRHS], p2.at[NRHS])

    def start(k, _):
        for p in range(4):
            q = [qs[p][k, :, tile(t)] for t in range(TILES)]
            fill(k, p, q, ds[p], keep if p == 0 else None, scale, source, one)
        return 0

    lax.fori_loop(0, K, start, 0, unroll=True)
    found = solve(source, scale, one, two)

    def finish(k, carry):
        upper, lower = carry
        images, here = local(found, ds, k)
        mask = owned(k, colour)
        up, low = 0.0, 0.0
        for p in range(4):
            for t in range(TILES):
                value = here[p][t]
                up = up + qs[p][k, :, tile(t)] * value
                low = low + images[p][t] * value
                if p == 0:
                    ch[k, :, tile(t)] = value
                else:
                    c[p - 1, k, :, tile(t)] = value
                if p < 2:
                    t2[p, k, :, tile(t)] = images[p][t]
                else:
                    t12[p - 2, k, :, tile(t)] = images[p][t]
        return upper + jnp.where(mask, up, 0.0), lower + jnp.where(mask, low, 0.0)

    zero = jnp.zeros((8, LANES), jnp.float32)
    upper, lower = lax.fori_loop(0, K, finish, (zero, zero), unroll=True)
    sums[0] = upper
    sums[1] = lower


def estimate(planes, passes):
    return pl.CostEstimate(
        flops=passes * 4 * K * 8 * NZ * 10, bytes_accessed=planes * K * 8 * NZ * 4, transcendentals=0
    )


def first_solve(r, joint, where, *arrays):
    return pl.pallas_call(
        functools.partial(first_kernel, r, joint),
        out_shape=([shape_of(3)] if joint else [shape_of(), shape_of(2)])
        + [shape_of(3), shape_of(2), jax.ShapeDtypeStruct((2, 8, LANES), jnp.float32)],
        in_specs=[SM] + [VM] * 5,
        out_specs=[VM] * (4 if joint else 5),
        scratch_shapes=SCRATCH,
        compiler_params=pltpu.CompilerParams(vmem_limit_bytes=VMEM_LIMIT),
        cost_estimate=estimate(16, SWEEPS + 1),
    )(where, *arrays)


def packed(values, out):
    rows = [jnp.sum(v, axis=0, keepdims=True) for v in values]
    rows += [jnp.zeros((1, LANES), jnp.float32)] * (16 - len(rows))
    totals = jnp.sum(jnp.concatenate(rows, axis=0), axis=1, keepdims=True)
    own = lax.broadcasted_iota(jnp.int32, (16, LANES), 0) == lax.broadcasted_iota(jnp.int32, (16, LANES), 1)
    line = jnp.sum(jnp.where(own, totals, 0.0), axis=0, keepdims=True)
    out[...] = jnp.broadcast_to(line, out.shape)


def plane_of(ref, i):
    return ref.at[i] if len(ref.shape) == 4 else ref


def join_kernel(where, *refs):
    cs, rights, sums, out = refs[:NRHS], refs[NRHS : 2 * NRHS], refs[2 * NRHS : 3 * NRHS], refs[-1]
    colour = where[0]
    zero = jnp.zeros((8, LANES), jnp.float32)
    uppers, lowers = [], []
    for r in range(NRHS):

        def body(k, total, r=r):
            add = 0.0
            for t in range(TILES):
                add = add + cs[r][2, k, :, tile(t)] * plane_of(rights[r], 0)[k, :, tile(t)]
            return total + jnp.where(owned(k, colour), add, 0.0)

        between = lax.fori_loop(0, K, body, zero, unroll=6)
        uppers.append(sums[r][0])
        lowers.append(sums[r][1] - 2.0 * between)
    packed(uppers + lowers, out)


def join(count, where, cs, rights, sums):
    return pl.pallas_call(
        join_kernel,
        out_shape=jax.ShapeDtypeStruct((count, LANES), jnp.float32),
        in_specs=[SM] + [VM] * (3 * NRHS),
        out_specs=VM,
        compiler_params=pltpu.CompilerParams(vmem_limit_bytes=VMEM_LIMIT),
        cost_estimate=estimate(12, 1),
    )(where, *cs, *rights, *sums)


def pick(table, index):
    line = jnp.sum(table[...], axis=0, keepdims=True)
    lane = lax.broadcasted_iota(jnp.int32, (1, LANES), 1)
    return jnp.sum(jnp.where(lane == index, line, 0.0), axis=1, keepdims=True)


def ratio(table, upper, lower):
    return pick(table, upper) / pick(table, lower)


def second_kernel(
    r, where, table, p1, p2, pd, ph, p4, c, cr, tr, t12,
    ca, cm, end, ta, tm, res, sums, scale, source, one, two,
):
    colour, device, count = where[0], where[1], where[2]
    keep = (device < count - 1).astype(jnp.float32)
    cd, td = end.at[0], end.at[1]
    cr = plane_of(cr, 0)
    if tr.shape[0] == 3:
        tr = tr.at[pl.ds(1, 2)]
    alpha = jnp.broadcast_to(ratio(table, r, NRHS + r), (8, LANES))
    which, place_at = halo(r)
    q1, q2, q3, q4 = p1.at[r], p2.at[r], (pd, ph)[which].at[place_at], p4.at[r]
    ds = (p1.at[NRHS], p2.at[NRHS], pd.at[0], p4.at[NRHS])

    def start(k, _):
        for p in range(4):
            values = []
            for t in range(TILES):
                if p == 0:
                    image = t12[0, k, :, tile(t)]
                    q = q1[k, :, tile(t)]
                elif p == 1:
                    image = t12[1, k, :, tile(t)] - cr[k, :, tile(t)]
                    q = q2[k, :, tile(t)]
                elif p == 2:
                    image = tr[0, k, :, tile(t)] - c[2, k, :, tile(t)]
                    q = q3[k, :, tile(t)]
                else:
                    image = tr[1, k, :, tile(t)]
                    q = q4[k, :, tile(t)]
                value = q - alpha * image
                res[p, k, :, tile(t)] = value
                values.append(value)
            fill(k, p, values, ds[p], keep if p == 3 else None, scale, source, one)
        return 0

    lax.fori_loop(0, K, start, 0, unroll=True)
    found = solve(source, scale, one, two)

    def finish(k, carry):
        images, here = local(found, ds, k)
        mask = owned(k, colour)
        adds = [0.0] * 5
        for p in range(4):
            for t in range(TILES):
                value, image, q = here[p][t], images[p][t], res[p, k, :, tile(t)]
                adds[0] = adds[0] + q * value
                adds[1] = adds[1] + image * value
                if p in (1, 2):
                    rest = q - image
                    adds[2] = adds[2] + rest * rest
                    adds[3] = adds[3] + rest * image
                    adds[4] = adds[4] + image * image
                    cm[p - 1, k, :, tile(t)] = value
                    tm[p - 1, k, :, tile(t)] = image
                else:
                    (ca if p == 0 else cd)[k, :, tile(t)] = value
                    (ta if p == 0 else td)[k, :, tile(t)] = image
        return tuple(a + jnp.where(mask, b, 0.0) for a, b in zip(carry, adds))

    zero = jnp.zeros((8, LANES), jnp.float32)
    found_sums = lax.fori_loop(0, K, finish, (zero,) * 5, unroll=True)
    for i in range(5):
        sums[i] = found_sums[i]


def second_solve(r, where, table, *arrays):
    return pl.pallas_call(
        functools.partial(second_kernel, r),
        out_shape=[
            shape_of(),
            shape_of(2),
            shape_of(2),
            shape_of(),
            shape_of(2),
            shape_of(4),
            jax.ShapeDtypeStruct((5, 8, LANES), jnp.float32),
        ],
        in_specs=[SM] + [VM] * 10,
        out_specs=[VM] * 7,
        scratch_shapes=SCRATCH,
        compiler_params=pltpu.CompilerParams(vmem_limit_bytes=VMEM_LIMIT),
        cost_estimate=estimate(28, SWEEPS + 1),
    )(where, table, *arrays)


def join_second_kernel(where, table, *refs):
    out = refs[-1]
    colour = where[0]
    zero = jnp.zeros((8, LANES), jnp.float32)
    rows = [[] for _ in range(5)]
    for r in range(NRHS):
        res, ca, ta, got, t2, sums = refs[1 + 6 * r : 7 + 6 * r]
        q0, t0, cl, tl = refs[0].at[r], t2.at[t2.shape[0] - 1], got.at[0], got.at[1]
        alpha = jnp.broadcast_to(ratio(table, r, NRHS + r), (8, LANES))

        def body(k, carry, res=res, ca=ca, ta=ta, cl=cl, tl=tl, q0=q0, t0=t0, alpha=alpha):
            adds = [0.0] * 4
            for t in range(TILES):
                at = (k, slice(None), tile(t))
                adds[0] = adds[0] + ca[at] * cl[at]
                for q, image in (
                    (q0[at] - alpha * t0[at], tl[at] - ca[at]),
                    (res[(0, *at)], ta[at] - cl[at]),
                ):
                    rest = q - image
                    adds[1] = adds[1] + rest * rest
                    adds[2] = adds[2] + rest * image
                    adds[3] = adds[3] + image * image
            mask = owned(k, colour)
            return tuple(a + jnp.where(mask, b, 0.0) for a, b in zip(carry, adds))

        between, *squares = lax.fori_loop(0, K, body, (zero,) * 4, unroll=6)
        rows[0].append(sums[0])
        rows[1].append(sums[1] - 2.0 * between)
        for i in range(3):
            rows[2 + i].append(sums[2 + i] + squares[i])
    packed([value for row in rows for value in row], out)


def join_second(count, where, table, arrays):
    return pl.pallas_call(
        join_second_kernel,
        out_shape=jax.ShapeDtypeStruct((count, LANES), jnp.float32),
        in_specs=[SM] + [VM] * (2 + 6 * NRHS),
        out_specs=VM,
        compiler_params=pltpu.CompilerParams(vmem_limit_bytes=VMEM_LIMIT),
        cost_estimate=estimate(40, 2),
    )(where, table, *arrays)


def pieces(r, alpha, refs, at):
    p0, t2, c, c3, res, got, ca, cm, ta, tm = refs
    q0, t0, c3, cl, tl = p0.at[r], t2.at[t2.shape[0] - 1], plane_of(c3, 0), got.at[0], got.at[1]
    return (
        [alpha * c[(p, *at)] for p in range(3)] + [alpha * c3[at]],
        [cl[at], ca[at], cm[(0, *at)], cm[(1, *at)]],
        [q0[at] - alpha * t0[at]] + [res[(p, *at)] for p in range(3)],
        [tl[at] - ca[at], ta[at] - cl[at], tm[(0, *at)], tm[(1, *at)]],
    )


def half_at(k, half, t):
    first = pl.multiple_of(half * (NZ // 2) + t * LANES, LANES)
    return k, slice(None), pl.ds(first, LANES)


def pack_kernel(r, where, table, *refs):
    *refs, out = refs
    other = 1 - where[0]
    alpha = jnp.broadcast_to(ratio(table, r, NRHS + r), (8, LANES))

    def body(k, _):
        for t in range(TILES // 2):
            for n, planes in enumerate(pieces(r, alpha, refs, half_at(k, other, t))):
                for p in range(4):
                    out[n, p, k, :, tile(t)] = planes[p]
        return 0

    lax.fori_loop(0, K, body, 0, unroll=6)


def pack(r, where, table, *arrays):
    return pl.pallas_call(
        functools.partial(pack_kernel, r),
        out_shape=jax.ShapeDtypeStruct((4, 4, K, 8, NZ // 2), jnp.float32),
        in_specs=[SM] + [VM] * 11,
        out_specs=VM,
        compiler_params=pltpu.CompilerParams(vmem_limit_bytes=VMEM_LIMIT),
        cost_estimate=estimate(16, 1),
    )(where, table, *arrays)


def last_kernel(where, table, after, *refs):
    norms, full_u, full_q, held, sems = refs[-5:]
    colour = where[0]
    rows = []
    pending = []
    for r in range(NRHS):
        theirs = refs[11 * r + 10]
        mine = refs[11 * r : 11 * r + 10]
        first = ratio(table, r, NRHS + r)
        second = ratio(after, r, NRHS + r)
        more = second - 1.0
        square, cross, own = (
            pick(after, i * NRHS + r) for i in (2, 3, 4)
        )
        total = square - 2.0 * more * cross + more * more * own
        rows.append(jnp.broadcast_to(jnp.sqrt(jnp.maximum(total, 0.0)), (1, LANES)))
        one = jnp.broadcast_to(first, (8, LANES))
        two = jnp.broadcast_to(second, (8, LANES))
        slot = r % 2
        if r >= 2:
            for copy in pending[r - 2]:
                copy.wait()

        def body(k, _, r=r, mine=mine, theirs=theirs, one=one, two=two, slot=slot):
            rows_at = pl.ds(k, 8, stride=K)
            for t in range(TILES // 2):
                at = (k, slice(None), tile(t))
                for side, (us, cs, qs, images) in enumerate(
                    (
                        pieces(r, one, mine, half_at(k, colour, t)),
                        [[theirs[(n, p, *at)] for p in range(4)] for n in range(4)],
                    )
                ):
                    for p in range(4):
                        held[slot, side, 0, p, t, rows_at, :] = us[p] + two * cs[p]
                        held[slot, side, 1, p, t, rows_at, :] = qs[p] - two * images[p]
            return 0

        lax.fori_loop(0, K, body, 0, unroll=6)
        copies = []
        for side, whose in enumerate((colour, 1 - colour)):
            low = pl.multiple_of(whose * (WIN - OWN), 8)
            start = pl.multiple_of(whose * OWN, 8)
            for n, full in enumerate((full_u, full_q)):
                for t in range(TILES // 2):
                    copies.append(
                        pltpu.make_async_copy(
                            held.at[slot, side, n, :, t, pl.ds(low, OWN), :],
                            full.at[r, :, pl.ds(start, OWN), tile(t)],
                            sems.at[slot, side, n, t],
                        )
                    )
        for copy in copies:
            copy.start()
        pending.append(copies)
    for copies in pending[max(0, NRHS - 2) :]:
        for copy in copies:
            copy.wait()
    rows += [jnp.zeros((1, LANES), jnp.float32)] * (8 - NRHS)
    norms[...] = jnp.concatenate(rows, axis=0)


def last(where, table, after, arrays):
    full = jax.ShapeDtypeStruct((NRHS, 4, NY, NZ // 2), jnp.float32)
    return pl.pallas_call(
        last_kernel,
        out_shape=[jax.ShapeDtypeStruct((8, LANES), jnp.float32), full, full],
        in_specs=[SM] + [VM] * (2 + 11 * NRHS),
        out_specs=[VM, HBM, HBM],
        scratch_shapes=[
            pltpu.VMEM((2, 2, 2, 4, TILES // 2, WIN, LANES), jnp.float32),
            pltpu.SemaphoreType.DMA((2, 2, 2, TILES // 2)),
        ],
        compiler_params=pltpu.CompilerParams(vmem_limit_bytes=VMEM_LIMIT),
        cost_estimate=estimate(70, 3),
    )(where, table, after, *arrays)


def everywhere(lines):
    return lax.all_to_all(lines, ("colour", *SUB), split_axis=0, concat_axis=0, tiled=True)


def shards(rhs, diagonal):
    colour = lax.axis_index("colour")
    device = lax.axis_index(SUB)
    total = lax.axis_size(SUB)
    devices = total * lax.axis_size("colour")
    forward = [(i, i + 1) for i in range(total - 1)]
    backward = [(i + 1, i) for i in range(total - 1)]
    where = jnp.stack([colour, device, jnp.int32(total)]).astype(jnp.int32)

    def right(value):
        return lax.ppermute(value, SUB, forward)

    def left(value):
        return lax.ppermute(value, SUB, backward)

    everything = range(NRHS + 1)
    (pd,) = prepare((((3, NRHS), (3, 0)),), where, rhs, diagonal)
    hd = right(pd)
    where, pd = lax.optimization_barrier((where, pd))
    ph, p0 = prepare(
        (tuple((3, r) for r in range(1, NRHS)), tuple((0, r) for r in everything)),
        where, rhs, diagonal,
    )
    hh = right(ph)
    p4 = left(p0)
    p1, p2 = prepare(tuple(tuple((plane, r) for r in everything) for plane in (1, 2)), where, rhs, diagonal)

    together, c0, inner0, sums0 = first_solve(0, True, where, hd, pd, p0, p1, p2)
    ahead = left(together)
    ch1, t1, c1, inner1, sums1 = first_solve(1, False, where, hd, hh, p0, p1, p2)
    ch1 = left(ch1)
    hh, p4 = lax.optimization_barrier((hh, p4))
    ch2, t2, c2, inner2, sums2 = first_solve(2, False, where, hd, hh, p0, p1, p2)
    ch2 = left(ch2)
    t = (together, t1, t2)
    c, cr = (c0, c1, c2), (ahead, ch1, ch2)
    inner = (inner0, inner1, inner2)
    table = everywhere(join(devices, where, c, cr, (sums0, sums1, sums2)))
    table, t1, t2 = lax.optimization_barrier((table, t1, t2))
    tr = (ahead, left(t1), left(t2))
    seconds = []
    sent = []
    for r in range(NRHS):
        out = second_solve(r, where, table, p1, p2, pd, ph, p4, c[r], cr[r], tr[r], inner[r])
        seconds.append(out)
        sent.append(right(out[2]))
    ca, cm, end, ta, tm, res, sums = zip(*seconds)
    got = sent
    arrays = [
        a
        for r in range(NRHS)
        for a in (res[r], ca[r], ta[r], got[r], t[r], sums[r])
    ]
    lines = join_second(devices, where, table, [p0, *arrays])
    pairs = [(0, 1), (1, 0)]
    arrays = []
    for r in range(NRHS):
        mine = [p0, t[r], c[r], cr[r], res[r], got[r], ca[r], cm[r], ta[r], tm[r]]
        half = pack(r, where, table, *mine)
        if r == NRHS - 1:
            lines, half = lax.optimization_barrier((lines, half))
        arrays += [*mine, lax.ppermute(half, "colour", pairs)]
    after = everywhere(lines)
    norms, full_u, full_q = last(where, table, after, arrays)
    return full_u, full_q, norms[:NRHS, 0]


def solution(mesh):
    torus = Mesh(
        mesh.devices.reshape(mesh.shape["colour"], 4, 4, 4), ("colour", "sub_0", "sub_1", "sub_2")
    )
    return jax.shard_map(
        shards,
        mesh=torus,
        in_specs=(P(None, SUB, None, None), P(SUB, None, None)),
        out_specs=(P(None, SUB, None, "colour"), P(None, SUB, None, "colour"), P()),
        check_vma=False,
    )
```

```python
import functools

import jax
import jax.numpy as jnp
from jax import lax
from jax.experimental import pallas as pl
from jax.experimental.pallas import tpu as pltpu
from jax.sharding import Mesh
from jax.sharding import PartitionSpec as P

OMEGA = 0.8
SWEEPS = 8
NY = 256
NZ = 512
NRHS = 3
OWN = 128
WIN = 144
K = WIN // 8
LANES = 128
TILES = NZ // LANES
SUB = ("sub_0", "sub_1", "sub_2")
VMEM_LIMIT = 12 * 1024 * 1024


def powers():
    total = [0.0] * SWEEPS
    power = [1.0]
    for _ in range(SWEEPS):
        for i, value in enumerate(power):
            total[i] += value
        longer = [0.0] * (len(power) + 1)
        for i, value in enumerate(power):
            longer[i] += (1.0 - OMEGA) * value
            longer[i + 1] += value
        power = longer
    return total


COEFFICIENTS = powers()
PLANE = (K, 8, NZ)
VM = pl.BlockSpec(memory_space=pltpu.VMEM)
SM = pl.BlockSpec(memory_space=pltpu.SMEM)
ANY = pl.BlockSpec(memory_space=pl.ANY)
HBM = pl.BlockSpec(memory_space=pltpu.MemorySpace.HBM)


def shape_of(*lead):
    return jax.ShapeDtypeStruct((*lead, *PLANE), jnp.float32)


def tile(t):
    return slice(t * LANES, (t + 1) * LANES)


def lanes():
    return lax.broadcasted_iota(jnp.int32, (8, LANES), 1)


def sublanes():
    return lax.broadcasted_iota(jnp.int32, (8, LANES), 0)


def owned(k, colour):
    row = sublanes() * K + k - colour * (WIN - OWN)
    return (row >= 0) & (row < OWN)


def close_edges(buf):
    sub = sublanes()
    for p in range(4):
        for t in range(TILES):
            last = pltpu.roll(buf[p, K, :, tile(t)], 1, 0)
            buf[p, 0, :, tile(t)] = jnp.where(sub == 0, 0.0, last)
            first = pltpu.roll(buf[p, 1, :, tile(t)], 7, 0)
            buf[p, K + 1, :, tile(t)] = jnp.where(sub == 7, 0.0, first)


def beside(buf, k):
    lane = lanes()
    first, last = lane == 0, lane == LANES - 1
    here = [[buf[p, k + 1, :, tile(t)] for t in range(TILES)] for p in range(4)]
    sums = []
    for p in range(4):
        up = [pltpu.roll(v, 1, 1) for v in here[p]]
        down = [pltpu.roll(v, LANES - 1, 1) for v in here[p]]
        row = []
        for t in range(TILES):
            total = jnp.where(first, up[t - 1] if t else 0.0, up[t])
            total = total + jnp.where(last, down[t + 1] if t + 1 < TILES else 0.0, down[t])
            total = total + (buf[p, k, :, tile(t)] + buf[p, k + 2, :, tile(t)])
            if p == 0:
                total = total + here[1][t]
            elif p == 3:
                total = total + here[2][t]
            else:
                total = total + (here[p - 1][t] + here[p + 1][t])
            row.append(total)
        sums.append(row)
    return sums, here


def solve(source, scale, one, two):
    close_edges(one)
    bufs = (one, two)
    for step, power in enumerate(range(SWEEPS - 2, -1, -1)):
        src, dst = bufs[step % 2], bufs[1 - step % 2]
        factor = COEFFICIENTS[power]

        def body(k, _, src=src, dst=dst, factor=factor):
            sums, _ = beside(src, k)
            for p in range(4):
                for t in range(TILES):
                    dst[p, k + 1, :, tile(t)] = (
                        scale[p, k, :, tile(t)] * sums[p][t]
                        + factor * source[p, k, :, tile(t)]
                    )
            return 0

        lax.fori_loop(0, K, body, 0, unroll=True)
        close_edges(dst)
    return bufs[(SWEEPS - 1) % 2]


def prepare_kernel(packs, where, rhs, diag, *refs):
    outs, (held, sem) = refs[: len(packs)], refs[len(packs) :]
    low = pl.multiple_of(where[0] * (NY - WIN), 8)
    places = [(out, i, *item) for out, pack in zip(outs, packs) for i, item in enumerate(pack)]
    copies = []
    for n, (_, _, plane, r) in enumerate(places):
        for t in range(TILES):
            if r < NRHS:
                src = rhs.at[r, plane, pl.ds(low, WIN), tile(t)]
            else:
                src = diag.at[plane, pl.ds(low, WIN), tile(t)]
            copies.append(pltpu.make_async_copy(src, held.at[n, t], sem.at[n, t]))
    for copy in copies:
        copy.start()
    for n, (out, i, _, _) in enumerate(places):
        for t in range(TILES):
            copies[n * TILES + t].wait()
            for k in range(K):
                out[i, k, :, tile(t)] = held[n, t, pl.ds(k, 8, stride=K), :]


def prepare(packs, where, rhs, diag):
    count = sum(len(pack) for pack in packs)
    return pl.pallas_call(
        functools.partial(prepare_kernel, packs),
        out_shape=[shape_of(len(pack)) for pack in packs],
        in_specs=[SM, HBM, HBM],
        out_specs=[VM] * len(packs),
        scratch_shapes=[
            pltpu.VMEM((count, TILES, WIN, LANES), jnp.float32),
            pltpu.SemaphoreType.DMA((count, TILES)),
        ],
        compiler_params=pltpu.CompilerParams(vmem_limit_bytes=VMEM_LIMIT),
        cost_estimate=pl.CostEstimate(flops=0, bytes_accessed=0, transcendentals=0),
    )(where, *(pltpu.with_memory_space_constraint(v, pltpu.MemorySpace.HBM) for v in (rhs, diag)))


def local(buf, diags, k):
    sums, here = beside(buf, k)
    images = [
        [(6.0 + diags[p][k, :, tile(t)]) * here[p][t] - sums[p][t] for t in range(TILES)]
        for p in range(4)
    ]
    return images, here


def fill(k, p, q, d, keep, scale, source, one):
    for t in range(TILES):
        s = OMEGA / (6.0 + d[k, :, tile(t)])
        if keep is not None:
            s = s * keep
        g = s * q[t]
        scale[p, k, :, tile(t)] = s
        source[p, k, :, tile(t)] = g
        one[p, k + 1, :, tile(t)] = g


SCRATCH = [
    pltpu.VMEM((4, K, 8, NZ), jnp.float32),
    pltpu.VMEM((4, K, 8, NZ), jnp.float32),
    pltpu.VMEM((4, K + 2, 8, NZ), jnp.float32),
    pltpu.VMEM((4, K + 2, 8, NZ), jnp.float32),
]


def halo(r):
    return (0, 1) if r == 0 else (1, r - 1)


def first_kernel(r, joint, where, pd, ph, p0, p1, p2, *refs):
    if joint:
        together, c, t12, sums, scale, source, one, two = refs
        ch, t2 = together.at[0], together.at[pl.ds(1, 2)]
    else:
        ch, t2, c, t12, sums, scale, source, one, two = refs
    colour, device = where[0], where[1]
    keep = (device > 0).astype(jnp.float32)
    which, at = halo(r)
    qs = ((pd, ph)[which].at[at], p0.at[r], p1.at[r], p2.at[r])
    ds = (pd.at[0], p0.at[NRHS], p1.at[NRHS], p2.at[NRHS])

    def start(k, _):
        for p in range(4):
            q = [qs[p][k, :, tile(t)] for t in range(TILES)]
            fill(k, p, q, ds[p], keep if p == 0 else None, scale, source, one)
        return 0

    lax.fori_loop(0, K, start, 0, unroll=True)
    found = solve(source, scale, one, two)

    def finish(k, carry):
        upper, lower = carry
        images, here = local(found, ds, k)
        mask = owned(k, colour)
        up, low = 0.0, 0.0
        for p in range(4):
            for t in range(TILES):
                value = here[p][t]
                up = up + qs[p][k, :, tile(t)] * value
                low = low + images[p][t] * value
                if p == 0:
                    ch[k, :, tile(t)] = value
                else:
                    c[p - 1, k, :, tile(t)] = value
                if p < 2:
                    t2[p, k, :, tile(t)] = images[p][t]
                else:
                    t12[p - 2, k, :, tile(t)] = images[p][t]
        return upper + jnp.where(mask, up, 0.0), lower + jnp.where(mask, low, 0.0)

    zero = jnp.zeros((8, LANES), jnp.float32)
    upper, lower = lax.fori_loop(0, K, finish, (zero, zero), unroll=True)
    sums[0] = upper
    sums[1] = lower


def estimate(planes, passes):
    return pl.CostEstimate(
        flops=passes * 4 * K * 8 * NZ * 10, bytes_accessed=planes * K * 8 * NZ * 4, transcendentals=0
    )


def first_solve(r, joint, where, *arrays):
    return pl.pallas_call(
        functools.partial(first_kernel, r, joint),
        out_shape=([shape_of(3)] if joint else [shape_of(), shape_of(2)])
        + [shape_of(3), shape_of(2), jax.ShapeDtypeStruct((2, 8, LANES), jnp.float32)],
        in_specs=[SM] + [VM] * 5,
        out_specs=[VM] * (4 if joint else 5),
        scratch_shapes=SCRATCH,
        compiler_params=pltpu.CompilerParams(vmem_limit_bytes=VMEM_LIMIT),
        cost_estimate=estimate(16, SWEEPS + 1),
    )(where, *arrays)


def packed(values, out):
    rows = [jnp.sum(v, axis=0, keepdims=True) for v in values]
    rows += [jnp.zeros((1, LANES), jnp.float32)] * (16 - len(rows))
    totals = jnp.sum(jnp.concatenate(rows, axis=0), axis=1, keepdims=True)
    own = lax.broadcasted_iota(jnp.int32, (16, LANES), 0) == lax.broadcasted_iota(jnp.int32, (16, LANES), 1)
    line = jnp.sum(jnp.where(own, totals, 0.0), axis=0, keepdims=True)
    out[...] = jnp.broadcast_to(line, out.shape)


def plane_of(ref, i):
    return ref.at[i] if len(ref.shape) == 4 else ref


def join_kernel(where, *refs):
    cs, rights, sums, out = refs[:NRHS], refs[NRHS : 2 * NRHS], refs[2 * NRHS : 3 * NRHS], refs[-1]
    colour = where[0]
    zero = jnp.zeros((8, LANES), jnp.float32)
    uppers, lowers = [], []
    for r in range(NRHS):

        def body(k, total, r=r):
            add = 0.0
            for t in range(TILES):
                add = add + cs[r][2, k, :, tile(t)] * plane_of(rights[r], 0)[k, :, tile(t)]
            return total + jnp.where(owned(k, colour), add, 0.0)

        between = lax.fori_loop(0, K, body, zero, unroll=6)
        uppers.append(sums[r][0])
        lowers.append(sums[r][1] - 2.0 * between)
    packed(uppers + lowers, out)


def join(count, where, cs, rights, sums):
    return pl.pallas_call(
        join_kernel,
        out_shape=jax.ShapeDtypeStruct((count, LANES), jnp.float32),
        in_specs=[SM] + [VM] * (3 * NRHS),
        out_specs=VM,
        compiler_params=pltpu.CompilerParams(vmem_limit_bytes=VMEM_LIMIT),
        cost_estimate=estimate(12, 1),
    )(where, *cs, *rights, *sums)


def pick(table, index):
    line = jnp.sum(table[...], axis=0, keepdims=True)
    lane = lax.broadcasted_iota(jnp.int32, (1, LANES), 1)
    return jnp.sum(jnp.where(lane == index, line, 0.0), axis=1, keepdims=True)


def ratio(table, upper, lower):
    return pick(table, upper) / pick(table, lower)


def second_kernel(
    r, where, table, p1, p2, pd, ph, p4, c, cr, tr, t12,
    ca, cm, end, ta, tm, res, sums, scale, source, one, two,
):
    colour, device, count = where[0], where[1], where[2]
    keep = (device < count - 1).astype(jnp.float32)
    cd, td = end.at[0], end.at[1]
    cr = plane_of(cr, 0)
    if tr.shape[0] == 3:
        tr = tr.at[pl.ds(1, 2)]
    alpha = jnp.broadcast_to(ratio(table, r, NRHS + r), (8, LANES))
    which, place_at = halo(r)
    q1, q2, q3, q4 = p1.at[r], p2.at[r], (pd, ph)[which].at[place_at], p4.at[r]
    ds = (p1.at[NRHS], p2.at[NRHS], pd.at[0], p4.at[NRHS])

    def start(k, _):
        for p in range(4):
            values = []
            for t in range(TILES):
                if p == 0:
                    image = t12[0, k, :, tile(t)]
                    q = q1[k, :, tile(t)]
                elif p == 1:
                    image = t12[1, k, :, tile(t)] - cr[k, :, tile(t)]
                    q = q2[k, :, tile(t)]
                elif p == 2:
                    image = tr[0, k, :, tile(t)] - c[2, k, :, tile(t)]
                    q = q3[k, :, tile(t)]
                else:
                    image = tr[1, k, :, tile(t)]
                    q = q4[k, :, tile(t)]
                value = q - alpha * image
                res[p, k, :, tile(t)] = value
                values.append(value)
            fill(k, p, values, ds[p], keep if p == 3 else None, scale, source, one)
        return 0

    lax.fori_loop(0, K, start, 0, unroll=True)
    found = solve(source, scale, one, two)

    def finish(k, carry):
        images, here = local(found, ds, k)
        mask = owned(k, colour)
        adds = [0.0] * 5
        for p in range(4):
            for t in range(TILES):
                value, image, q = here[p][t], images[p][t], res[p, k, :, tile(t)]
                adds[0] = adds[0] + q * value
                adds[1] = adds[1] + image * value
                if p in (1, 2):
                    rest = q - image
                    adds[2] = adds[2] + rest * rest
                    adds[3] = adds[3] + rest * image
                    adds[4] = adds[4] + image * image
                    cm[p - 1, k, :, tile(t)] = value
                    tm[p - 1, k, :, tile(t)] = image
                else:
                    (ca if p == 0 else cd)[k, :, tile(t)] = value
                    (ta if p == 0 else td)[k, :, tile(t)] = image
        return tuple(a + jnp.where(mask, b, 0.0) for a, b in zip(carry, adds))

    zero = jnp.zeros((8, LANES), jnp.float32)
    found_sums = lax.fori_loop(0, K, finish, (zero,) * 5, unroll=True)
    for i in range(5):
        sums[i] = found_sums[i]


def second_solve(r, where, table, *arrays):
    return pl.pallas_call(
        functools.partial(second_kernel, r),
        out_shape=[
            shape_of(),
            shape_of(2),
            shape_of(2),
            shape_of(),
            shape_of(2),
            shape_of(4),
            jax.ShapeDtypeStruct((5, 8, LANES), jnp.float32),
        ],
        in_specs=[SM] + [VM] * 10,
        out_specs=[VM] * 7,
        scratch_shapes=SCRATCH,
        compiler_params=pltpu.CompilerParams(vmem_limit_bytes=VMEM_LIMIT),
        cost_estimate=estimate(28, SWEEPS + 1),
    )(where, table, *arrays)


def join_second_kernel(where, table, *refs):
    out = refs[-1]
    colour = where[0]
    zero = jnp.zeros((8, LANES), jnp.float32)
    rows = [[] for _ in range(5)]
    for r in range(NRHS):
        res, ca, ta, got, t2, sums = refs[1 + 6 * r : 7 + 6 * r]
        q0, t0, cl, tl = refs[0].at[r], t2.at[t2.shape[0] - 1], got.at[0], got.at[1]
        alpha = jnp.broadcast_to(ratio(table, r, NRHS + r), (8, LANES))

        def body(k, carry, res=res, ca=ca, ta=ta, cl=cl, tl=tl, q0=q0, t0=t0, alpha=alpha):
            adds = [0.0] * 4
            for t in range(TILES):
                at = (k, slice(None), tile(t))
                adds[0] = adds[0] + ca[at] * cl[at]
                for q, image in (
                    (q0[at] - alpha * t0[at], tl[at] - ca[at]),
                    (res[(0, *at)], ta[at] - cl[at]),
                ):
                    rest = q - image
                    adds[1] = adds[1] + rest * rest
                    adds[2] = adds[2] + rest * image
                    adds[3] = adds[3] + image * image
            mask = owned(k, colour)
            return tuple(a + jnp.where(mask, b, 0.0) for a, b in zip(carry, adds))

        between, *squares = lax.fori_loop(0, K, body, (zero,) * 4, unroll=6)
        rows[0].append(sums[0])
        rows[1].append(sums[1] - 2.0 * between)
        for i in range(3):
            rows[2 + i].append(sums[2 + i] + squares[i])
    packed([value for row in rows for value in row], out)


def join_second(count, where, table, arrays):
    return pl.pallas_call(
        join_second_kernel,
        out_shape=jax.ShapeDtypeStruct((count, LANES), jnp.float32),
        in_specs=[SM] + [VM] * (2 + 6 * NRHS),
        out_specs=VM,
        compiler_params=pltpu.CompilerParams(vmem_limit_bytes=VMEM_LIMIT),
        cost_estimate=estimate(40, 2),
    )(where, table, *arrays)


def pieces(r, alpha, refs, at):
    p0, t2, c, c3, res, got, ca, cm, ta, tm = refs
    q0, t0, c3, cl, tl = p0.at[r], t2.at[t2.shape[0] - 1], plane_of(c3, 0), got.at[0], got.at[1]
    return (
        [alpha * c[(p, *at)] for p in range(3)] + [alpha * c3[at]],
        [cl[at], ca[at], cm[(0, *at)], cm[(1, *at)]],
        [q0[at] - alpha * t0[at]] + [res[(p, *at)] for p in range(3)],
        [tl[at] - ca[at], ta[at] - cl[at], tm[(0, *at)], tm[(1, *at)]],
    )


def half_at(k, half, t):
    first = pl.multiple_of(half * (NZ // 2) + t * LANES, LANES)
    return k, slice(None), pl.ds(first, LANES)


def pack_kernel(r, where, table, *refs):
    *refs, out = refs
    other = 1 - where[0]
    alpha = jnp.broadcast_to(ratio(table, r, NRHS + r), (8, LANES))

    def body(k, _):
        for t in range(TILES // 2):
            for n, planes in enumerate(pieces(r, alpha, refs, half_at(k, other, t))):
                for p in range(4):
                    out[n, p, k, :, tile(t)] = planes[p]
        return 0

    lax.fori_loop(0, K, body, 0, unroll=6)


def pack(r, where, table, *arrays):
    return pl.pallas_call(
        functools.partial(pack_kernel, r),
        out_shape=jax.ShapeDtypeStruct((4, 4, K, 8, NZ // 2), jnp.float32),
        in_specs=[SM] + [VM] * 11,
        out_specs=VM,
        compiler_params=pltpu.CompilerParams(vmem_limit_bytes=VMEM_LIMIT),
        cost_estimate=estimate(16, 1),
    )(where, table, *arrays)


def last_kernel(where, table, after, *refs):
    norms, full_u, full_q, held, sems = refs[-5:]
    colour = where[0]
    rows = []
    pending = []
    for r in range(NRHS):
        theirs = refs[11 * r + 10]
        mine = refs[11 * r : 11 * r + 10]
        first = ratio(table, r, NRHS + r)
        second = ratio(after, r, NRHS + r)
        more = second - 1.0
        square, cross, own = (
            pick(after, i * NRHS + r) for i in (2, 3, 4)
        )
        total = square - 2.0 * more * cross + more * more * own
        rows.append(jnp.broadcast_to(jnp.sqrt(jnp.maximum(total, 0.0)), (1, LANES)))
        one = jnp.broadcast_to(first, (8, LANES))
        two = jnp.broadcast_to(second, (8, LANES))
        slot = r % 2
        if r >= 2:
            for copy in pending[r - 2]:
                copy.wait()

        def body(k, _, r=r, mine=mine, theirs=theirs, one=one, two=two, slot=slot):
            rows_at = pl.ds(k, 8, stride=K)
            for t in range(TILES // 2):
                at = (k, slice(None), tile(t))
                for side, (us, cs, qs, images) in enumerate(
                    (
                        pieces(r, one, mine, half_at(k, colour, t)),
                        [[theirs[(n, p, *at)] for p in range(4)] for n in range(4)],
                    )
                ):
                    for p in range(4):
                        held[slot, side, 0, p, t, rows_at, :] = us[p] + two * cs[p]
                        held[slot, side, 1, p, t, rows_at, :] = qs[p] - two * images[p]
            return 0

        lax.fori_loop(0, K, body, 0, unroll=6)
        copies = []
        for side, whose in enumerate((colour, 1 - colour)):
            low = pl.multiple_of(whose * (WIN - OWN), 8)
            start = pl.multiple_of(whose * OWN, 8)
            for n, full in enumerate((full_u, full_q)):
                for t in range(TILES // 2):
                    copies.append(
                        pltpu.make_async_copy(
                            held.at[slot, side, n, :, t, pl.ds(low, OWN), :],
                            full.at[r, :, pl.ds(start, OWN), tile(t)],
                            sems.at[slot, side, n, t],
                        )
                    )
        for copy in copies:
            copy.start()
        pending.append(copies)
    for copies in pending[max(0, NRHS - 2) :]:
        for copy in copies:
            copy.wait()
    rows += [jnp.zeros((1, LANES), jnp.float32)] * (8 - NRHS)
    norms[...] = jnp.concatenate(rows, axis=0)


def last(where, table, after, arrays):
    full = jax.ShapeDtypeStruct((NRHS, 4, NY, NZ // 2), jnp.float32)
    return pl.pallas_call(
        last_kernel,
        out_shape=[jax.ShapeDtypeStruct((8, LANES), jnp.float32), full, full],
        in_specs=[SM] + [VM] * (2 + 11 * NRHS),
        out_specs=[VM, HBM, HBM],
        scratch_shapes=[
            pltpu.VMEM((2, 2, 2, 4, TILES // 2, WIN, LANES), jnp.float32),
            pltpu.SemaphoreType.DMA((2, 2, 2, TILES // 2)),
        ],
        compiler_params=pltpu.CompilerParams(vmem_limit_bytes=VMEM_LIMIT),
        cost_estimate=estimate(70, 3),
    )(where, table, after, *arrays)


def everywhere(lines):
    return lax.all_to_all(lines, ("colour", *SUB), split_axis=0, concat_axis=0, tiled=True)


def shards(rhs, diagonal):
    colour = lax.axis_index("colour")
    device = lax.axis_index(SUB)
    total = lax.axis_size(SUB)
    devices = total * lax.axis_size("colour")
    forward = [(i, i + 1) for i in range(total - 1)]
    backward = [(i + 1, i) for i in range(total - 1)]
    where = jnp.stack([colour, device, jnp.int32(total)]).astype(jnp.int32)

    def right(value):
        return lax.ppermute(value, SUB, forward)

    def left(value):
        return lax.ppermute(value, SUB, backward)

    everything = range(NRHS + 1)
    pd, ph, p0 = prepare(
        (
            ((3, NRHS), (3, 0)),
            tuple((3, r) for r in range(1, NRHS)),
            tuple((0, r) for r in everything),
        ),
        where, rhs, diagonal,
    )
    hd, hh = right(pd), right(ph)
    p4 = left(p0)
    p1, p2 = prepare(tuple(tuple((plane, r) for r in everything) for plane in (1, 2)), where, rhs, diagonal)

    together, c0, inner0, sums0 = first_solve(0, True, where, hd, pd, p0, p1, p2)
    ahead = left(together)
    ch1, t1, c1, inner1, sums1 = first_solve(1, False, where, hd, hh, p0, p1, p2)
    ch1 = left(ch1)
    hh, p4 = lax.optimization_barrier((hh, p4))
    ch2, t2, c2, inner2, sums2 = first_solve(2, False, where, hd, hh, p0, p1, p2)
    ch2 = left(ch2)
    t = (together, t1, t2)
    c, cr = (c0, c1, c2), (ahead, ch1, ch2)
    inner = (inner0, inner1, inner2)
    table = everywhere(join(devices, where, c, cr, (sums0, sums1, sums2)))
    table, t1, t2 = lax.optimization_barrier((table, t1, t2))
    tr = (ahead, left(t1), left(t2))
    seconds = []
    sent = []
    for r in range(NRHS):
        out = second_solve(r, where, table, p1, p2, pd, ph, p4, c[r], cr[r], tr[r], inner[r])
        seconds.append(out)
        sent.append(right(out[2]))
    ca, cm, end, ta, tm, res, sums = zip(*seconds)
    got = sent
    arrays = [
        a
        for r in range(NRHS)
        for a in (res[r], ca[r], ta[r], got[r], t[r], sums[r])
    ]
    lines = join_second(devices, where, table, [p0, *arrays])
    pairs = [(0, 1), (1, 0)]
    arrays = []
    for r in range(NRHS):
        mine = [p0, t[r], c[r], cr[r], res[r], got[r], ca[r], cm[r], ta[r], tm[r]]
        half = pack(r, where, table, *mine)
        if r == NRHS - 1:
            lines, half = lax.optimization_barrier((lines, half))
        arrays += [*mine, lax.ppermute(half, "colour", pairs)]
    after = everywhere(lines)
    norms, full_u, full_q = last(where, table, after, arrays)
    return full_u, full_q, norms[:NRHS, 0]


def solution(mesh):
    torus = Mesh(
        mesh.devices.reshape(mesh.shape["colour"], 4, 4, 4), ("colour", "sub_0", "sub_1", "sub_2")
    )
    return jax.shard_map(
        shards,
        mesh=torus,
        in_specs=(P(None, SUB, None, None), P(SUB, None, None)),
        out_specs=(P(None, SUB, None, "colour"), P(None, SUB, None, "colour"), P()),
        check_vma=False,
    )
```

```python
import functools

import jax
import jax.numpy as jnp
from jax import lax
from jax.experimental import pallas as pl
from jax.experimental.pallas import tpu as pltpu
from jax.sharding import Mesh
from jax.sharding import PartitionSpec as P

OMEGA = 0.8
SWEEPS = 8
NY = 256
NZ = 512
NRHS = 3
OWN = 128
WIN = 144
K = WIN // 8
LANES = 128
TILES = NZ // LANES
SUB = ("sub_0", "sub_1", "sub_2")
VMEM_LIMIT = 12 * 1024 * 1024


def powers():
    total = [0.0] * SWEEPS
    power = [1.0]
    for _ in range(SWEEPS):
        for i, value in enumerate(power):
            total[i] += value
        longer = [0.0] * (len(power) + 1)
        for i, value in enumerate(power):
            longer[i] += (1.0 - OMEGA) * value
            longer[i + 1] += value
        power = longer
    return total


COEFFICIENTS = powers()
PLANE = (K, 8, NZ)
VM = pl.BlockSpec(memory_space=pltpu.VMEM)
SM = pl.BlockSpec(memory_space=pltpu.SMEM)
ANY = pl.BlockSpec(memory_space=pl.ANY)
HBM = pl.BlockSpec(memory_space=pltpu.MemorySpace.HBM)


def shape_of(*lead):
    return jax.ShapeDtypeStruct((*lead, *PLANE), jnp.float32)


def tile(t):
    return slice(t * LANES, (t + 1) * LANES)


def lanes():
    return lax.broadcasted_iota(jnp.int32, (8, LANES), 1)


def sublanes():
    return lax.broadcasted_iota(jnp.int32, (8, LANES), 0)


def owned(k, colour):
    row = sublanes() * K + k - colour * (WIN - OWN)
    return (row >= 0) & (row < OWN)


def close_edges(buf):
    sub = sublanes()
    for p in range(4):
        for t in range(TILES):
            last = pltpu.roll(buf[p, K, :, tile(t)], 1, 0)
            buf[p, 0, :, tile(t)] = jnp.where(sub == 0, 0.0, last)
            first = pltpu.roll(buf[p, 1, :, tile(t)], 7, 0)
            buf[p, K + 1, :, tile(t)] = jnp.where(sub == 7, 0.0, first)


def beside(buf, k):
    lane = lanes()
    first, last = lane == 0, lane == LANES - 1
    here = [[buf[p, k + 1, :, tile(t)] for t in range(TILES)] for p in range(4)]
    sums = []
    for p in range(4):
        up = [pltpu.roll(v, 1, 1) for v in here[p]]
        down = [pltpu.roll(v, LANES - 1, 1) for v in here[p]]
        row = []
        for t in range(TILES):
            total = jnp.where(first, up[t - 1] if t else 0.0, up[t])
            total = total + jnp.where(last, down[t + 1] if t + 1 < TILES else 0.0, down[t])
            total = total + (buf[p, k, :, tile(t)] + buf[p, k + 2, :, tile(t)])
            if p == 0:
                total = total + here[1][t]
            elif p == 3:
                total = total + here[2][t]
            else:
                total = total + (here[p - 1][t] + here[p + 1][t])
            row.append(total)
        sums.append(row)
    return sums, here


def solve(source, scale, one, two):
    close_edges(one)
    bufs = (one, two)
    for step, power in enumerate(range(SWEEPS - 2, -1, -1)):
        src, dst = bufs[step % 2], bufs[1 - step % 2]
        factor = COEFFICIENTS[power]

        def body(k, _, src=src, dst=dst, factor=factor):
            sums, _ = beside(src, k)
            for p in range(4):
                for t in range(TILES):
                    dst[p, k + 1, :, tile(t)] = (
                        scale[p, k, :, tile(t)] * sums[p][t]
                        + factor * source[p, k, :, tile(t)]
                    )
            return 0

        lax.fori_loop(0, K, body, 0, unroll=True)
        close_edges(dst)
    return bufs[(SWEEPS - 1) % 2]


def prepare_kernel(packs, where, rhs, diag, *refs):
    outs, (held, sem) = refs[: len(packs)], refs[len(packs) :]
    low = pl.multiple_of(where[0] * (NY - WIN), 8)
    places = [(out, i, *item) for out, pack in zip(outs, packs) for i, item in enumerate(pack)]
    copies = []
    for n, (_, _, plane, r) in enumerate(places):
        for t in range(TILES):
            if r < NRHS:
                src = rhs.at[r, plane, pl.ds(low, WIN), tile(t)]
            else:
                src = diag.at[plane, pl.ds(low, WIN), tile(t)]
            copies.append(pltpu.make_async_copy(src, held.at[n, t], sem.at[n, t]))
    for copy in copies:
        copy.start()
    for n, (out, i, _, _) in enumerate(places):
        for t in range(TILES):
            copies[n * TILES + t].wait()
            for k in range(K):
                out[i, k, :, tile(t)] = held[n, t, pl.ds(k, 8, stride=K), :]


def prepare(packs, where, rhs, diag):
    count = sum(len(pack) for pack in packs)
    return pl.pallas_call(
        functools.partial(prepare_kernel, packs),
        out_shape=[shape_of(len(pack)) for pack in packs],
        in_specs=[SM, HBM, HBM],
        out_specs=[VM] * len(packs),
        scratch_shapes=[
            pltpu.VMEM((count, TILES, WIN, LANES), jnp.float32),
            pltpu.SemaphoreType.DMA((count, TILES)),
        ],
        compiler_params=pltpu.CompilerParams(vmem_limit_bytes=VMEM_LIMIT),
        cost_estimate=pl.CostEstimate(flops=0, bytes_accessed=0, transcendentals=0),
    )(where, *(pltpu.with_memory_space_constraint(v, pltpu.MemorySpace.HBM) for v in (rhs, diag)))


def local(buf, diags, k):
    sums, here = beside(buf, k)
    images = [
        [(6.0 + diags[p][k, :, tile(t)]) * here[p][t] - sums[p][t] for t in range(TILES)]
        for p in range(4)
    ]
    return images, here


def fill(k, p, q, d, keep, scale, source, one):
    for t in range(TILES):
        s = OMEGA / (6.0 + d[k, :, tile(t)])
        if keep is not None:
            s = s * keep
        g = s * q[t]
        scale[p, k, :, tile(t)] = s
        source[p, k, :, tile(t)] = g
        one[p, k + 1, :, tile(t)] = g


SCRATCH = [
    pltpu.VMEM((4, K, 8, NZ), jnp.float32),
    pltpu.VMEM((4, K, 8, NZ), jnp.float32),
    pltpu.VMEM((4, K + 2, 8, NZ), jnp.float32),
    pltpu.VMEM((4, K + 2, 8, NZ), jnp.float32),
]


def halo(r):
    return (0, 1) if r == 0 else (1, r - 1)


def first_kernel(r, joint, where, pd, ph, p0, p1, p2, *refs):
    if joint:
        together, c, t12, sums, scale, source, one, two = refs
        ch, t2 = together.at[0], together.at[pl.ds(1, 2)]
    else:
        ch, t2, c, t12, sums, scale, source, one, two = refs
    colour, device = where[0], where[1]
    keep = (device > 0).astype(jnp.float32)
    which, at = halo(r)
    qs = ((pd, ph)[which].at[at], p0.at[r], p1.at[r], p2.at[r])
    ds = (pd.at[0], p0.at[NRHS], p1.at[NRHS], p2.at[NRHS])

    def start(k, _):
        for p in range(4):
            q = [qs[p][k, :, tile(t)] for t in range(TILES)]
            fill(k, p, q, ds[p], keep if p == 0 else None, scale, source, one)
        return 0

    lax.fori_loop(0, K, start, 0, unroll=True)
    found = solve(source, scale, one, two)

    def finish(k, carry):
        upper, lower = carry
        images, here = local(found, ds, k)
        mask = owned(k, colour)
        up, low = 0.0, 0.0
        for p in range(4):
            for t in range(TILES):
                value = here[p][t]
                up = up + qs[p][k, :, tile(t)] * value
                low = low + images[p][t] * value
                if p == 0:
                    ch[k, :, tile(t)] = value
                else:
                    c[p - 1, k, :, tile(t)] = value
                if p < 2:
                    t2[p, k, :, tile(t)] = images[p][t]
                else:
                    t12[p - 2, k, :, tile(t)] = images[p][t]
        return upper + jnp.where(mask, up, 0.0), lower + jnp.where(mask, low, 0.0)

    zero = jnp.zeros((8, LANES), jnp.float32)
    upper, lower = lax.fori_loop(0, K, finish, (zero, zero), unroll=True)
    sums[0] = upper
    sums[1] = lower


def estimate(planes, passes):
    return pl.CostEstimate(
        flops=passes * 4 * K * 8 * NZ * 10, bytes_accessed=planes * K * 8 * NZ * 4, transcendentals=0
    )


def first_solve(r, joint, where, *arrays):
    return pl.pallas_call(
        functools.partial(first_kernel, r, joint),
        out_shape=([shape_of(3)] if joint else [shape_of(), shape_of(2)])
        + [shape_of(3), shape_of(2), jax.ShapeDtypeStruct((2, 8, LANES), jnp.float32)],
        in_specs=[SM] + [VM] * 5,
        out_specs=[VM] * (4 if joint else 5),
        scratch_shapes=SCRATCH,
        compiler_params=pltpu.CompilerParams(vmem_limit_bytes=VMEM_LIMIT),
        cost_estimate=estimate(16, SWEEPS + 1),
    )(where, *arrays)


def packed(values, out):
    rows = [jnp.sum(v, axis=0, keepdims=True) for v in values]
    rows += [jnp.zeros((1, LANES), jnp.float32)] * (16 - len(rows))
    totals = jnp.sum(jnp.concatenate(rows, axis=0), axis=1, keepdims=True)
    own = lax.broadcasted_iota(jnp.int32, (16, LANES), 0) == lax.broadcasted_iota(jnp.int32, (16, LANES), 1)
    line = jnp.sum(jnp.where(own, totals, 0.0), axis=0, keepdims=True)
    out[...] = jnp.broadcast_to(line, out.shape)


def plane_of(ref, i):
    return ref.at[i] if len(ref.shape) == 4 else ref


def join_kernel(where, *refs):
    cs, rights, sums, out = refs[:NRHS], refs[NRHS : 2 * NRHS], refs[2 * NRHS : 3 * NRHS], refs[-1]
    colour = where[0]
    zero = jnp.zeros((8, LANES), jnp.float32)
    uppers, lowers = [], []
    for r in range(NRHS):

        def body(k, total, r=r):
            add = 0.0
            for t in range(TILES):
                add = add + cs[r][2, k, :, tile(t)] * plane_of(rights[r], 0)[k, :, tile(t)]
            return total + jnp.where(owned(k, colour), add, 0.0)

        between = lax.fori_loop(0, K, body, zero, unroll=True)
        uppers.append(sums[r][0])
        lowers.append(sums[r][1] - 2.0 * between)
    packed(uppers + lowers, out)


def join(count, where, cs, rights, sums):
    return pl.pallas_call(
        join_kernel,
        out_shape=jax.ShapeDtypeStruct((count, LANES), jnp.float32),
        in_specs=[SM] + [VM] * (3 * NRHS),
        out_specs=VM,
        compiler_params=pltpu.CompilerParams(vmem_limit_bytes=VMEM_LIMIT),
        cost_estimate=estimate(12, 1),
    )(where, *cs, *rights, *sums)


def pick(table, index):
    line = jnp.sum(table[...], axis=0, keepdims=True)
    lane = lax.broadcasted_iota(jnp.int32, (1, LANES), 1)
    return jnp.sum(jnp.where(lane == index, line, 0.0), axis=1, keepdims=True)


def ratio(table, upper, lower):
    return pick(table, upper) / pick(table, lower)


def second_kernel(
    r, where, table, p1, p2, pd, ph, p4, c, cr, tr, t12,
    ca, cm, end, ta, tm, res, sums, scale, source, one, two,
):
    colour, device, count = where[0], where[1], where[2]
    keep = (device < count - 1).astype(jnp.float32)
    cd, td = end.at[0], end.at[1]
    cr = plane_of(cr, 0)
    if tr.shape[0] == 3:
        tr = tr.at[pl.ds(1, 2)]
    alpha = jnp.broadcast_to(ratio(table, r, NRHS + r), (8, LANES))
    which, place_at = halo(r)
    q1, q2, q3, q4 = p1.at[r], p2.at[r], (pd, ph)[which].at[place_at], p4.at[r]
    ds = (p1.at[NRHS], p2.at[NRHS], pd.at[0], p4.at[NRHS])

    def start(k, _):
        for p in range(4):
            values = []
            for t in range(TILES):
                if p == 0:
                    image = t12[0, k, :, tile(t)]
                    q = q1[k, :, tile(t)]
                elif p == 1:
                    image = t12[1, k, :, tile(t)] - cr[k, :, tile(t)]
                    q = q2[k, :, tile(t)]
                elif p == 2:
                    image = tr[0, k, :, tile(t)] - c[2, k, :, tile(t)]
                    q = q3[k, :, tile(t)]
                else:
                    image = tr[1, k, :, tile(t)]
                    q = q4[k, :, tile(t)]
                value = q - alpha * image
                res[p, k, :, tile(t)] = value
                values.append(value)
            fill(k, p, values, ds[p], keep if p == 3 else None, scale, source, one)
        return 0

    lax.fori_loop(0, K, start, 0, unroll=True)
    found = solve(source, scale, one, two)

    def finish(k, carry):
        images, here = local(found, ds, k)
        mask = owned(k, colour)
        adds = [0.0] * 5
        for p in range(4):
            for t in range(TILES):
                value, image, q = here[p][t], images[p][t], res[p, k, :, tile(t)]
                adds[0] = adds[0] + q * value
                adds[1] = adds[1] + image * value
                if p in (1, 2):
                    rest = q - image
                    adds[2] = adds[2] + rest * rest
                    adds[3] = adds[3] + rest * image
                    adds[4] = adds[4] + image * image
                    cm[p - 1, k, :, tile(t)] = value
                    tm[p - 1, k, :, tile(t)] = image
                else:
                    (ca if p == 0 else cd)[k, :, tile(t)] = value
                    (ta if p == 0 else td)[k, :, tile(t)] = image
        return tuple(a + jnp.where(mask, b, 0.0) for a, b in zip(carry, adds))

    zero = jnp.zeros((8, LANES), jnp.float32)
    found_sums = lax.fori_loop(0, K, finish, (zero,) * 5, unroll=True)
    for i in range(5):
        sums[i] = found_sums[i]


def second_solve(r, where, table, *arrays):
    return pl.pallas_call(
        functools.partial(second_kernel, r),
        out_shape=[
            shape_of(),
            shape_of(2),
            shape_of(2),
            shape_of(),
            shape_of(2),
            shape_of(4),
            jax.ShapeDtypeStruct((5, 8, LANES), jnp.float32),
        ],
        in_specs=[SM] + [VM] * 10,
        out_specs=[VM] * 7,
        scratch_shapes=SCRATCH,
        compiler_params=pltpu.CompilerParams(vmem_limit_bytes=VMEM_LIMIT),
        cost_estimate=estimate(28, SWEEPS + 1),
    )(where, table, *arrays)


def join_second_kernel(where, table, *refs):
    out = refs[-1]
    colour = where[0]
    zero = jnp.zeros((8, LANES), jnp.float32)
    rows = [[] for _ in range(5)]
    for r in range(NRHS):
        res, ca, ta, got, t2, sums = refs[1 + 6 * r : 7 + 6 * r]
        q0, t0, cl, tl = refs[0].at[r], t2.at[t2.shape[0] - 1], got.at[0], got.at[1]
        alpha = jnp.broadcast_to(ratio(table, r, NRHS + r), (8, LANES))

        def body(k, carry, res=res, ca=ca, ta=ta, cl=cl, tl=tl, q0=q0, t0=t0, alpha=alpha):
            adds = [0.0] * 4
            for t in range(TILES):
                at = (k, slice(None), tile(t))
                adds[0] = adds[0] + ca[at] * cl[at]
                for q, image in (
                    (q0[at] - alpha * t0[at], tl[at] - ca[at]),
                    (res[(0, *at)], ta[at] - cl[at]),
                ):
                    rest = q - image
                    adds[1] = adds[1] + rest * rest
                    adds[2] = adds[2] + rest * image
                    adds[3] = adds[3] + image * image
            mask = owned(k, colour)
            return tuple(a + jnp.where(mask, b, 0.0) for a, b in zip(carry, adds))

        between, *squares = lax.fori_loop(0, K, body, (zero,) * 4, unroll=True)
        rows[0].append(sums[0])
        rows[1].append(sums[1] - 2.0 * between)
        for i in range(3):
            rows[2 + i].append(sums[2 + i] + squares[i])
    packed([value for row in rows for value in row], out)


def join_second(count, where, table, arrays):
    return pl.pallas_call(
        join_second_kernel,
        out_shape=jax.ShapeDtypeStruct((count, LANES), jnp.float32),
        in_specs=[SM] + [VM] * (2 + 6 * NRHS),
        out_specs=VM,
        compiler_params=pltpu.CompilerParams(vmem_limit_bytes=VMEM_LIMIT),
        cost_estimate=estimate(40, 2),
    )(where, table, *arrays)


def pieces(r, alpha, refs, at):
    p0, t2, c, c3, res, got, ca, cm, ta, tm = refs
    q0, t0, c3, cl, tl = p0.at[r], t2.at[t2.shape[0] - 1], plane_of(c3, 0), got.at[0], got.at[1]
    return (
        [alpha * c[(p, *at)] for p in range(3)] + [alpha * c3[at]],
        [cl[at], ca[at], cm[(0, *at)], cm[(1, *at)]],
        [q0[at] - alpha * t0[at]] + [res[(p, *at)] for p in range(3)],
        [tl[at] - ca[at], ta[at] - cl[at], tm[(0, *at)], tm[(1, *at)]],
    )


def half_at(k, half, t):
    first = pl.multiple_of(half * (NZ // 2) + t * LANES, LANES)
    return k, slice(None), pl.ds(first, LANES)


def pack_kernel(r, where, table, *refs):
    *refs, out = refs
    other = 1 - where[0]
    alpha = jnp.broadcast_to(ratio(table, r, NRHS + r), (8, LANES))

    def body(k, _):
        for t in range(TILES // 2):
            for n, planes in enumerate(pieces(r, alpha, refs, half_at(k, other, t))):
                for p in range(4):
                    out[n, p, k, :, tile(t)] = planes[p]
        return 0

    lax.fori_loop(0, K, body, 0, unroll=9)


def pack(r, where, table, *arrays):
    return pl.pallas_call(
        functools.partial(pack_kernel, r),
        out_shape=jax.ShapeDtypeStruct((4, 4, K, 8, NZ // 2), jnp.float32),
        in_specs=[SM] + [VM] * 11,
        out_specs=VM,
        compiler_params=pltpu.CompilerParams(vmem_limit_bytes=VMEM_LIMIT),
        cost_estimate=estimate(16, 1),
    )(where, table, *arrays)


def last_kernel(where, table, after, *refs):
    norms, full_u, full_q, held, sems = refs[-5:]
    colour = where[0]
    rows = []
    pending = []
    for r in range(NRHS):
        theirs = refs[11 * r + 10]
        mine = refs[11 * r : 11 * r + 10]
        first = ratio(table, r, NRHS + r)
        second = ratio(after, r, NRHS + r)
        more = second - 1.0
        square, cross, own = (
            pick(after, i * NRHS + r) for i in (2, 3, 4)
        )
        total = square - 2.0 * more * cross + more * more * own
        rows.append(jnp.broadcast_to(jnp.sqrt(jnp.maximum(total, 0.0)), (1, LANES)))
        one = jnp.broadcast_to(first, (8, LANES))
        two = jnp.broadcast_to(second, (8, LANES))
        slot = r % 2
        if r >= 2:
            for copy in pending[r - 2]:
                copy.wait()

        def body(k, _, r=r, mine=mine, theirs=theirs, one=one, two=two, slot=slot):
            rows_at = pl.ds(k, 8, stride=K)
            for t in range(TILES // 2):
                at = (k, slice(None), tile(t))
                for side, (us, cs, qs, images) in enumerate(
                    (
                        pieces(r, one, mine, half_at(k, colour, t)),
                        [[theirs[(n, p, *at)] for p in range(4)] for n in range(4)],
                    )
                ):
                    for p in range(4):
                        held[slot, side, 0, p, t, rows_at, :] = us[p] + two * cs[p]
                        held[slot, side, 1, p, t, rows_at, :] = qs[p] - two * images[p]
            return 0

        lax.fori_loop(0, K, body, 0, unroll=9)
        copies = []
        for side, whose in enumerate((colour, 1 - colour)):
            low = pl.multiple_of(whose * (WIN - OWN), 8)
            start = pl.multiple_of(whose * OWN, 8)
            for n, full in enumerate((full_u, full_q)):
                for t in range(TILES // 2):
                    copies.append(
                        pltpu.make_async_copy(
                            held.at[slot, side, n, :, t, pl.ds(low, OWN), :],
                            full.at[r, :, pl.ds(start, OWN), tile(t)],
                            sems.at[slot, side, n, t],
                        )
                    )
        for copy in copies:
            copy.start()
        pending.append(copies)
    for copies in pending[max(0, NRHS - 2) :]:
        for copy in copies:
            copy.wait()
    rows += [jnp.zeros((1, LANES), jnp.float32)] * (8 - NRHS)
    norms[...] = jnp.concatenate(rows, axis=0)


def last(where, table, after, arrays):
    full = jax.ShapeDtypeStruct((NRHS, 4, NY, NZ // 2), jnp.float32)
    return pl.pallas_call(
        last_kernel,
        out_shape=[jax.ShapeDtypeStruct((8, LANES), jnp.float32), full, full],
        in_specs=[SM] + [VM] * (2 + 11 * NRHS),
        out_specs=[VM, HBM, HBM],
        scratch_shapes=[
            pltpu.VMEM((2, 2, 2, 4, TILES // 2, WIN, LANES), jnp.float32),
            pltpu.SemaphoreType.DMA((2, 2, 2, TILES // 2)),
        ],
        compiler_params=pltpu.CompilerParams(vmem_limit_bytes=VMEM_LIMIT),
        cost_estimate=estimate(70, 3),
    )(where, table, after, *arrays)


def everywhere(lines):
    return lax.all_to_all(lines, ("colour", *SUB), split_axis=0, concat_axis=0, tiled=True)


def shards(rhs, diagonal):
    colour = lax.axis_index("colour")
    device = lax.axis_index(SUB)
    total = lax.axis_size(SUB)
    devices = total * lax.axis_size("colour")
    forward = [(i, i + 1) for i in range(total - 1)]
    backward = [(i + 1, i) for i in range(total - 1)]
    where = jnp.stack([colour, device, jnp.int32(total)]).astype(jnp.int32)

    def right(value):
        return lax.ppermute(value, SUB, forward)

    def left(value):
        return lax.ppermute(value, SUB, backward)

    everything = range(NRHS + 1)
    pd, ph, p0 = prepare(
        (
            ((3, NRHS), (3, 0)),
            tuple((3, r) for r in range(1, NRHS)),
            tuple((0, r) for r in everything),
        ),
        where, rhs, diagonal,
    )
    hd, hh = right(pd), right(ph)
    p4 = left(p0)
    p1, p2 = prepare(tuple(tuple((plane, r) for r in everything) for plane in (1, 2)), where, rhs, diagonal)

    together, c0, inner0, sums0 = first_solve(0, True, where, hd, pd, p0, p1, p2)
    ahead = left(together)
    ch1, t1, c1, inner1, sums1 = first_solve(1, False, where, hd, hh, p0, p1, p2)
    ch1 = left(ch1)
    hh, p4 = lax.optimization_barrier((hh, p4))
    ch2, t2, c2, inner2, sums2 = first_solve(2, False, where, hd, hh, p0, p1, p2)
    ch2 = left(ch2)
    t = (together, t1, t2)
    c, cr = (c0, c1, c2), (ahead, ch1, ch2)
    inner = (inner0, inner1, inner2)
    table = everywhere(join(devices, where, c, cr, (sums0, sums1, sums2)))
    table, t1, t2 = lax.optimization_barrier((table, t1, t2))
    tr = (ahead, left(t1), left(t2))
    seconds = []
    sent = []
    for r in range(NRHS):
        out = second_solve(r, where, table, p1, p2, pd, ph, p4, c[r], cr[r], tr[r], inner[r])
        seconds.append(out)
        sent.append(right(out[2]))
    ca, cm, end, ta, tm, res, sums = zip(*seconds)
    got = sent
    arrays = [
        a
        for r in range(NRHS)
        for a in (res[r], ca[r], ta[r], got[r], t[r], sums[r])
    ]
    lines = join_second(devices, where, table, [p0, *arrays])
    pairs = [(0, 1), (1, 0)]
    arrays = []
    for r in range(NRHS):
        mine = [p0, t[r], c[r], cr[r], res[r], got[r], ca[r], cm[r], ta[r], tm[r]]
        half = pack(r, where, table, *mine)
        if r == NRHS - 1:
            lines, half = lax.optimization_barrier((lines, half))
        arrays += [*mine, lax.ppermute(half, "colour", pairs)]
    after = everywhere(lines)
    norms, full_u, full_q = last(where, table, after, arrays)
    return full_u, full_q, norms[:NRHS, 0]


def solution(mesh):
    torus = Mesh(
        mesh.devices.reshape(mesh.shape["colour"], 4, 4, 4), ("colour", "sub_0", "sub_1", "sub_2")
    )
    return jax.shard_map(
        shards,
        mesh=torus,
        in_specs=(P(None, SUB, None, None), P(SUB, None, None)),
        out_specs=(P(None, SUB, None, "colour"), P(None, SUB, None, "colour"), P()),
        check_vma=False,
    )
```
